32 devices in a mesh: mem: 4 (over y, core), ctx: 8 (over z, x).
Axes of the slice: x: 2, y: 2, z: 4, core: 2. Of those that a mesh axis runs over, the one named last changes fastest.
Arguments:
- queries: bfloat16 [8, 512, 32, 128], P('ctx', 'mem'), may hold values from -6 to 6
- keys: bfloat16 [8, 512, 32, 128], P('ctx', 'mem'), may hold values from -6 to 6
- values: bfloat16 [8, 512, 32, 128], P('ctx', 'mem'), may hold values from -6 to 6
- log_decay: bfloat16 [8, 512, 32], P('ctx', 'mem'), may hold values from -1 to 0, as said below
- routes: int32 [8, 512, 2], P('ctx', 'mem'), may hold values from 0 to 3, all different within a row; in each aligned block of 128 rows (0 to 127, 128 to 255, ..., all dimensions but the last counted through in order) at most 72 rows name the same one
- route_weight: float32 [8, 512, 2], P('ctx', 'mem'), may hold values from 0.2 to 1
- gain: float32 [4096], replicated, may hold values from 0.25 to 1.75
Outputs:
- layer_out: bfloat16 [8, 512, 32, 128], P('ctx', 'mem')
The draws below stay inside these ranges and needn't reach their ends.
Inputs may be any that keep to these rules, and one draw needn't show every extreme that they name: `routes`: A token's two memories differ. Among the tokens of one device (an aligned block of 128 tokens) no memory is named by more than 72 tokens, and in some such block a memory is named by exactly 72. `log_decay`: entries are negative.
All inputs are finite; a program needn't handle non-finite values.
Results may differ from the reference program's by a relative error of at most 0.015.
Values may be sent and summed in bfloat16 or wider, within the bound.
No kernel may reach another device: no remote copies, remote signals or barrier semaphores. Data moves between devices by JAX's collectives and lax.ppermute only.
A program may use at most 128 MiB of HBM per device.

```python
import math
import jax
import jax.numpy as jnp
import numpy as np
from jax import lax

HEAD_COUNT = 32
HD = 128
TOP = 2
TOK_DEV = 128
MEM = 4
CAP = 72
BLOCK_TOKENS = 512
BLOCK_COUNT = 8
WINDOW_TOKENS = 4096
HH = 4096


def draw_log_decay(key, part):
    parallel_flows = jax.random.split(jax.random.fold_in(key, 11), 7)
    fast_count = HEAD_COUNT // 2
    order = jax.random.permutation(parallel_flows[0], HEAD_COUNT)
    gentle_decay = order >= fast_count
    slow_rate = jnp.exp(jax.random.uniform(parallel_flows[1], (HEAD_COUNT,), jnp.float32, math.log(0.1), math.log(0.8))) / (WINDOW_TOKENS // 2)
    fast_rate = jnp.exp(jax.random.uniform(parallel_flows[2], (HEAD_COUNT,), jnp.float32, math.log(0.05), math.log(0.08)))
    base = jnp.where(gentle_decay, slow_rate, fast_rate)
    block_factor = jnp.exp(jax.random.uniform(parallel_flows[3], (BLOCK_COUNT, 1, HEAD_COUNT), jnp.float32, math.log(0.6), math.log(1.6)))
    token_factor = jnp.exp(jax.random.uniform(parallel_flows[4], (BLOCK_COUNT, BLOCK_TOKENS, HEAD_COUNT), jnp.float32, math.log(0.5), math.log(1.5)))
    rate = base[None, None, :] * block_factor * token_factor
    spike_position = jax.random.randint(parallel_flows[5], (3,), 0, WINDOW_TOKENS)
    token_offsets = jnp.arange(WINDOW_TOKENS).reshape(BLOCK_COUNT, BLOCK_TOKENS)
    spike_active = jnp.any(token_offsets[:, :, None] == spike_position[None, None, :], axis=-1)
    spike_length = jax.random.uniform(parallel_flows[6], (BLOCK_COUNT, BLOCK_TOKENS, HEAD_COUNT), jnp.float32, math.log(0.5), math.log(0.8))
    additional_term = jnp.where(spike_active[:, :, None] & gentle_decay[None, None, :], spike_length, 0.0)
    return (additional_term - rate).astype(jnp.bfloat16)


def shard_levels(stream_key, shape, pieces, least, largest):
    factor_of = 1.0
    for axis_at, shards_of in pieces:
        draws = jax.random.uniform(jax.random.fold_in(jax.random.fold_in(stream_key, 6), axis_at), (shards_of,), jnp.float32, least / len(pieces), largest / len(pieces))
        factor_of = factor_of * jnp.repeat(jnp.exp(draws), shape[axis_at] // shards_of).reshape((-1,) + (1,) * (len(shape) - 1 - axis_at))
    return factor_of


def routed_block(stream_key, own, number, rows, amount, top, reach, slope):
    ranking = jax.random.permutation(stream_key, amount)
    crowded, usual = portions_of(amount, rows * top, reach, slope, True), portions_of(amount, rows * top, reach, slope, False)
    places = jnp.arange(amount)

    def named(lengths, offset_by):
        used = int((lengths > 0).sum())
        fixed = max(1, used // 4)
        moved = fixed + (places - fixed + offset_by * (used - fixed)) % max(1, amount - fixed)
        return jnp.zeros((amount,), jnp.int32).at[ranking[jnp.where(places < fixed, places, moved)]].set(jnp.asarray(lengths, jnp.int32))

    lengths = jnp.where(number % 4 == 0, named(crowded, number // 4), named(usual, number - number // 4 - 1))
    mixed = jax.random.permutation(jax.random.fold_in(own, 3), amount)
    giver, sink = mixed[0:amount // 2 * 2:2], mixed[1:amount // 2 * 2:2]
    margin = jnp.minimum(lengths[giver] - 1, reach - lengths[sink]) // 2
    margin = jnp.where((giver == ranking[0]) | (sink == ranking[0]) | (lengths[sink] == 0), 0, jnp.maximum(margin, 0))
    moved = jax.random.randint(jax.random.fold_in(own, 4), (amount // 2,), 0, 1 << 20) % (margin + 1)
    lengths = lengths.at[giver].add(-moved).at[sink].add(moved)
    members = jnp.searchsorted(jnp.cumsum(lengths), jnp.arange(rows * top), side="right").astype(jnp.int32)
    listing = members.reshape(top, rows).T
    listing = listing[jax.random.permutation(jax.random.fold_in(own, 1), rows)]
    offset_by = jax.random.randint(jax.random.fold_in(own, 2), (rows, 1), 0, top)
    return jnp.take_along_axis(listing, (jnp.arange(top)[None, :] + offset_by) % top, axis=1)


def portions_of(number_of, total, reach, slope, full):
    weights = [(1 << 20) // math.isqrt(grade ** slope) + 1 for grade in range(1, number_of + 1)]
    largest = reach if full else min(reach, max(-(-total // number_of), total * weights[0] // sum(weights)))
    least = 1 if total - largest >= number_of - 1 else 0
    holding, rest = [largest] + [least] * (number_of - 1), total - largest - least * (number_of - 1)
    while rest > 0:
        free = [i for i in range(1, number_of) if holding[i] < largest] or [i for i in range(1, number_of) if holding[i] < reach]
        pool, remaining = sum([weights[i] for i in free]), rest
        for i in free:
            addition = min(reach - holding[i], max(1, remaining * weights[i] // pool), rest)
            holding[i] = holding[i] + addition
            rest = rest - addition
    return np.array(holding)


def centred(own_key, extent, width, bound, shards=(), kind=jnp.bfloat16):
    factor_of = shard_levels(own_key, extent, shards, -0.22, 0.18) if shards else 1.0
    values = jax.random.normal(own_key, extent, jnp.float32) * width * factor_of
    return jnp.minimum(jnp.maximum(values, -bound), bound).astype(kind)


def setup_inputs(seed: int = 0) -> dict:
    arg_keys = jax.random.split(jax.random.key(seed), 8)
    queries = centred(arg_keys[0], (BLOCK_COUNT, BLOCK_TOKENS, HEAD_COUNT, HD), 1.0, 6.0, ((0, 8), (1, 4)))
    keys = centred(arg_keys[1], (BLOCK_COUNT, BLOCK_TOKENS, HEAD_COUNT, HD), 1.0, 6.0, ((0, 8), (1, 4)))
    values = centred(arg_keys[2], (BLOCK_COUNT, BLOCK_TOKENS, HEAD_COUNT, HD), 1.0, 6.0, ((0, 8), (1, 4)))
    log_decay = draw_log_decay(jax.random.fold_in(arg_keys[7], 71), 0)
    routes_keys = jax.random.split(jax.random.fold_in(arg_keys[4], 1), BLOCK_COUNT * BLOCK_TOKENS // TOK_DEV)
    routes_turns = jax.random.permutation(jax.random.fold_in(arg_keys[4], 3), BLOCK_COUNT * BLOCK_TOKENS // TOK_DEV)
    routes = jax.vmap(lambda own, number: routed_block(jax.random.fold_in(arg_keys[4], 2), own, number, TOK_DEV, MEM, TOP, CAP, 2))(routes_keys, routes_turns).reshape((BLOCK_COUNT, BLOCK_TOKENS, TOP))
    route_weight = jnp.clip(0.2 + 0.8 * jax.random.uniform(arg_keys[5], (BLOCK_COUNT, BLOCK_TOKENS, TOP), jnp.float32) ** shard_levels(arg_keys[5], (BLOCK_COUNT, BLOCK_TOKENS, TOP), ((0, 8), (1, 4)), -0.2, 0.2), 0.2, 1.0)
    gain = jnp.clip(1.0 + 0.15 * jax.random.normal(arg_keys[6], (HH,), jnp.float32), 0.25, 1.75)
    return dict(queries=queries, keys=keys, values=values, log_decay=log_decay, routes=routes, route_weight=route_weight, gain=gain)


def block_output(query_block_rows, key_block_rows, value_block_rows, block_rate, entering_state, query_scale):
    running_decay = jnp.cumsum(block_rate.astype(jnp.float32), axis=0)
    head_cumul = running_decay.T
    diff = head_cumul[:, :, None] - head_cumul[:, None, :]
    count_rows = query_block_rows.shape[0]
    causal = jnp.arange(count_rows)[:, None] >= jnp.arange(count_rows)[None, :]
    scores = jnp.einsum('ihd,jhd->hij', query_block_rows.astype(jnp.float32), key_block_rows.astype(jnp.float32), precision=lax.Precision.HIGHEST)
    weights = (jnp.where(causal, jnp.exp(jnp.where(causal, diff, 0.0)), 0.0) * scores * query_scale).astype(jnp.bfloat16)
    intra = jnp.einsum('hij,jhd->ihd', weights.astype(jnp.float32), value_block_rows.astype(jnp.float32), precision=lax.Precision.HIGHEST)
    across_block_output = jnp.einsum('epm,pmx->epx', query_block_rows.astype(jnp.float32), entering_state, precision=lax.Precision.HIGHEST) * (jnp.exp(running_decay) * query_scale)[:, :, None]
    readout = (intra + across_block_output).astype(jnp.bfloat16)
    total = running_decay[-1]
    retained_mask = jnp.exp(total[None, :] - running_decay)
    state_increment = jnp.einsum('dyn,dye->yne', key_block_rows.astype(jnp.float32) * retained_mask[:, :, None], value_block_rows.astype(jnp.float32), precision=lax.Precision.HIGHEST)
    state_out = jnp.exp(total)[:, None, None] * entering_state + state_increment
    return (readout, state_out)

def head_norm(rows):
    square_mean = lax.optimization_barrier(jnp.mean(rows * rows, axis=-1, keepdims=True))
    return rows * lax.rsqrt(square_mean + 1e-06)

def reference(queries, keys, values, log_decay, routes, route_weight, gain):
    slots = MEM * CAP
    query_scale = HD ** (-0.5)
    slot_ids = jnp.arange(slots, dtype=jnp.int32)
    token_offsets = jnp.arange(BLOCK_TOKENS, dtype=jnp.int32)
    gain_heads = gain.reshape(HEAD_COUNT, HD).astype(jnp.float32)

    def one_block(states, block):
        query_block_rows, key_block_rows, value_block_rows, block_rate, block_route, block_weight = block

        def one_memory(memory):
            named = block_route == memory
            member = jnp.any(named, axis=1)
            counted = member.astype(jnp.int32)
            rank = jnp.cumsum(counted) - counted
            match = member[None, :] & (rank[None, :] == slot_ids[:, None])
            source = lax.optimization_barrier(jnp.sum(jnp.where(match, token_offsets[None, :], 0), axis=1)).astype(jnp.int32)
            filled = jnp.any(match, axis=1)

            def packed(table):
                shaped = filled.reshape((-1,) + (1,) * (table.ndim - 1))
                return jnp.where(shaped, table[source], jnp.zeros((), table.dtype))
            readout, new_state = block_output(packed(query_block_rows), packed(key_block_rows), packed(value_block_rows), packed(block_rate), states[memory], query_scale)
            token_out = head_norm(readout[jnp.minimum(rank, slots - 1).astype(jnp.int32)].astype(jnp.float32))
            weight = lax.optimization_barrier(jnp.sum(jnp.where(named, block_weight, 0.0), axis=1))
            term = jnp.where(member[:, None, None], token_out, 0.0) * weight[:, None, None]
            return (term, new_state)
        terms, new_states = lax.map(one_memory, jnp.arange(MEM, dtype=jnp.int32))
        mixed = lax.optimization_barrier(jnp.sum(terms, axis=0))
        return (new_states, (mixed * gain_heads).astype(jnp.bfloat16))
    initial = jnp.zeros((MEM, HEAD_COUNT, HD, HD), jnp.float32)
    final_states, outputs = lax.scan(one_block, initial, (queries, keys, values, log_decay, routes, route_weight))
    return outputs
```

```python
import functools

import jax
import jax.numpy as jnp
from jax import lax
from jax.experimental import pallas as pl
from jax.experimental.pallas import tpu as pltpu
from jax.sharding import Mesh
from jax.sharding import PartitionSpec as P

F32 = jnp.float32
BF16 = jnp.bfloat16
META = 16
ROWS = 8


def dot(a, b, dims=((1,), (0,))):
    return lax.dot_general(a, b, (dims, ((), ())), preferred_element_type=F32)


def pack_kernel(hl, td, q_ref, k_ref, v_ref, ld_ref, rt_ref, wt_ref, kv_out, q_out, scr, ld_scr):
    i = pl.program_id(0)
    hb = q_ref.shape[1]
    hd = q_ref.shape[2]

    @pl.when(i == 0)
    def _():
        ld_scr[...] = ld_ref[...].astype(F32)

    for src, out, base in ((k_ref, kv_out, 0), (v_ref, kv_out, hl * td), (q_ref, q_out, 0)):
        scr[...] = src[...].astype(F32).reshape(td * hb, hd)
        for j in range(hb):
            rows = scr[pl.ds(j, td, stride=hb), :].astype(BF16)
            start = base + (j % hl) * td
            out[j // hl, start : start + td, :] = rows
    w = wt_ref[...]
    hi = w.astype(BF16).astype(F32)
    mid = (w - hi).astype(BF16).astype(F32)
    low = (w - hi) - mid
    table = jnp.concatenate([rt_ref[...].astype(F32), hi, mid, low], axis=0)
    here = ld_scr[pl.ds(pl.multiple_of(i * hb, hb), hb), :]
    for dd in range(hb // hl):
        own = here if dd == 0 else pltpu.roll(here, hb - dd * hl, 0)
        kv_out[dd, 2 * hl * td :, :] = jnp.concatenate([table, own], axis=0).astype(BF16)


def pack(queries, keys, values, ld_t, routes_t, weight_t, g, hl):
    td, heads, hd = queries.shape
    hb = 8
    per = hb // hl
    rows = 2 * hl * td + META
    whole = lambda a: pl.BlockSpec(a.shape, lambda i: (0,) * a.ndim)
    block = pl.BlockSpec((td, hb, hd), lambda i: (0, i, 0))
    return pl.pallas_call(
        functools.partial(pack_kernel, hl, td),
        grid=(heads // hb,),
        in_specs=[block, block, block, whole(ld_t), whole(routes_t), whole(weight_t)],
        out_specs=[
            pl.BlockSpec((per, rows, hd), lambda i: (i, 0, 0)),
            pl.BlockSpec((per, hl * td, hd), lambda i: (i, 0, 0)),
        ],
        out_shape=[
            jax.ShapeDtypeStruct((g, rows, hd), BF16),
            jax.ShapeDtypeStruct((g, hl * td, hd), BF16),
        ],
        scratch_shapes=[pltpu.VMEM((td * hb, hd), F32), pltpu.VMEM((heads, td), F32)],
        name="pack",
    )(queries, keys, values, ld_t, routes_t, weight_t)


def meta_rows(kv_ref, s, hl, memories, base):
    meta = kv_ref[s, base:, :].astype(F32)
    td = meta.shape[1]
    row = lax.broadcasted_iota(jnp.int32, (ROWS, td), 0)
    memory = lax.rem(row, memories).astype(F32)
    first = meta[0:1] == memory
    second = meta[1:2] == memory
    rate = jnp.broadcast_to(meta[8:9], (ROWS, td))
    for h in range(1, hl):
        rate = jnp.where(row >= h * memories, meta[8 + h : 9 + h], rate)
    member = first | second
    return meta, first, second, member, jnp.where(member, rate, 0.0)


def running_sums(kv_ref, a_scr, cs_scr, g, hl, memories, base):
    td = a_scr.shape[1]
    for s in range(g):
        a_scr[s * ROWS : (s + 1) * ROWS, :] = meta_rows(kv_ref, s, hl, memories, base)[4]
    t0 = lax.broadcasted_iota(jnp.int32, (td, 2 * td), 0)
    t1 = lax.broadcasted_iota(jnp.int32, (td, 2 * td), 1)
    upper = jnp.where(t0 <= t1, 1.0, 0.0).astype(BF16)
    cs_scr[...] = dot(a_scr[...].astype(BF16), upper)


def state_kernel(g, hl, memories, td, kv_ref, state_ref, total_ref, a_scr, cs_scr, dec_scr, acc_scr):
    hd = kv_ref.shape[2]
    base = 2 * hl * td
    running_sums(kv_ref, a_scr, cs_scr, g, hl, memories, base)
    after = jnp.zeros((ROWS, td), F32)
    for s in reversed(range(g)):
        member = meta_rows(kv_ref, s, hl, memories, base)[3]
        rows = slice(s * ROWS, (s + 1) * ROWS)
        running, total = cs_scr[rows, :td], cs_scr[rows, td:]
        dec_scr[s] = jnp.where(member, jnp.exp(total - running + after), 0.0)
        after = after + total
    total_ref[...] = jnp.exp(after)
    acc_scr[...] = jnp.zeros_like(acc_scr)

    def chunk(s, carry):
        columns = dec_scr[s].T
        for h in range(hl):
            key = kv_ref[s, h * td : (h + 1) * td, :]
            value = kv_ref[s, (hl + h) * td : (hl + h + 1) * td, :].astype(F32)
            scaled = jnp.concatenate(
                [
                    (value * columns[:, h * memories + m : h * memories + m + 1]).astype(BF16)
                    for m in range(memories)
                ],
                axis=1,
            )
            acc_scr[h] += dot(key, scaled, ((0,), (0,)))
        return carry

    lax.fori_loop(0, g, chunk, 0)
    state_ref[...] = acc_scr[...].astype(BF16)


def local_state(kv, hl, memories, td):
    g, rows, hd = kv.shape
    return pl.pallas_call(
        functools.partial(state_kernel, g, hl, memories, td),
        in_specs=[pl.BlockSpec(memory_space=pltpu.VMEM)],
        out_specs=[pl.BlockSpec(memory_space=pltpu.VMEM)] * 2,
        out_shape=[
            jax.ShapeDtypeStruct((hl, hd, memories * hd), BF16),
            jax.ShapeDtypeStruct((ROWS, td), F32),
        ],
        scratch_shapes=[
            pltpu.VMEM((g * ROWS, td), F32),
            pltpu.VMEM((g * ROWS, 2 * td), F32),
            pltpu.VMEM((g, ROWS, td), F32),
            pltpu.VMEM((hl, hd, memories * hd), F32),
        ],
        cost_estimate=pl.CostEstimate(
            flops=2 * g * td * hl * memories * hd * hd, bytes_accessed=kv.size * 2, transcendentals=0
        ),
        name="local_state",
    )(kv)


def readout_kernel(
    g, hl, memories, td, q_ref, kv_ref, state_ref, gain_ref, out_ref, a_scr, cs_scr, col_scr, fac_scr, st_scr
):
    hd = kv_ref.shape[2]
    base = 2 * hl * td
    scale = hd ** (-0.5)
    running_sums(kv_ref, a_scr, cs_scr, g, hl, memories, base)
    half_after = jnp.ones((ROWS, td), F32)
    for s in reversed(range(g)):
        meta, first, second, member, _ = meta_rows(kv_ref, s, hl, memories, base)
        rows = slice(s * ROWS, (s + 1) * ROWS)
        running, half = cs_scr[rows, :td], 0.5 * cs_scr[rows, td:]
        weight = [meta[2 + i : 3 + i] + (meta[4 + i : 5 + i] + meta[6 + i : 7 + i]) for i in range(2)]
        col_scr[s, 0:ROWS, :] = jnp.where(member, jnp.exp(half - running), 0.0)
        col_scr[s, ROWS : 2 * ROWS, :] = jnp.exp(running - half) * scale
        col_scr[s, 2 * ROWS :, :] = jnp.where(first, weight[0], 0.0) + jnp.where(second, weight[1], 0.0)
        own = jnp.exp(half)
        fac_scr[s, 0:ROWS, :] = own
        fac_scr[s, ROWS:, :] = half_after
        half_after = own
    for h in range(hl):
        for m in range(memories):
            j = h * memories + m
            lanes = slice(m * hd, (m + 1) * hd)
            st_scr[h, :, lanes] = state_ref[h, :, lanes].astype(F32) * half_after[j : j + 1, :]
    ones = jnp.full((hd, hd), 1.0 / hd, F32).astype(BF16)
    causal = lax.broadcasted_iota(jnp.int32, (td, td), 0) >= lax.broadcasted_iota(jnp.int32, (td, td), 1)

    def chunk(s, carry):
        columns = col_scr[s].T
        factors = fac_scr[s]
        for h in range(hl):
            query = q_ref[s, h * td : (h + 1) * td, :]
            key = kv_ref[s, h * td : (h + 1) * td, :]
            value = kv_ref[s, (hl + h) * td : (hl + h + 1) * td, :].astype(F32)
            scores = jnp.where(causal, dot(query, key, ((1,), (1,))), 0.0).astype(BF16)
            scaled = jnp.concatenate(
                [
                    (value * columns[:, h * memories + m : h * memories + m + 1]).astype(BF16)
                    for m in range(memories)
                ],
                axis=1,
            )
            state = st_scr[h]
            left = jnp.concatenate([scores, query], axis=1)
            right = jnp.concatenate([scaled, state.astype(BF16)], axis=0)
            read = dot(left, right)
            grown = state + dot(key, scaled, ((0,), (0,)))
            mixed = jnp.zeros((td, hd), F32)
            for m in range(memories):
                j = h * memories + m
                lanes = slice(m * hd, (m + 1) * hd)
                st_scr[h, :, lanes] = (
                    grown[:, lanes] * factors[j : j + 1, :] * factors[ROWS + j : ROWS + j + 1, :]
                )
                rows_out = read[:, lanes] * columns[:, ROWS + j : ROWS + j + 1]
                mean = dot((rows_out * rows_out).astype(BF16), ones)
                mixed = mixed + rows_out * (
                    lax.rsqrt(mean + 1e-06) * columns[:, 2 * ROWS + j : 2 * ROWS + j + 1]
                )
            out_ref[s, h * td : (h + 1) * td, :] = (mixed * gain_ref[h : h + 1, :]).astype(BF16)
        return carry

    lax.fori_loop(0, g, chunk, 0)


def readout(q, kv, state, gain, hl, memories, td):
    g, rows, hd = kv.shape
    return pl.pallas_call(
        functools.partial(readout_kernel, g, hl, memories, td),
        in_specs=[pl.BlockSpec(memory_space=pltpu.VMEM)] * 4,
        out_specs=pl.BlockSpec(memory_space=pltpu.VMEM),
        out_shape=jax.ShapeDtypeStruct(q.shape, BF16),
        scratch_shapes=[
            pltpu.VMEM((g * ROWS, td), F32),
            pltpu.VMEM((g * ROWS, 2 * td), F32),
            pltpu.VMEM((g, 3 * ROWS, td), F32),
            pltpu.VMEM((g, 2 * ROWS, td), F32),
            pltpu.VMEM((hl, hd, memories * hd), F32),
        ],
        cost_estimate=pl.CostEstimate(
            flops=8 * g * td * hl * memories * hd * hd, bytes_accessed=kv.size * 4, transcendentals=0
        ),
        name="readout",
    )(q, kv, state, gain)


def entering_state(state, total, groups, hl, memories):
    if groups == 1:
        return jnp.zeros_like(state)
    state = lax.ppermute(state, "hi", [(i, i + 1) for i in range(groups - 1)])
    if groups == 2:
        return state
    factor = lax.ppermute(total[:, :1], "hi", [(i, i + 1) for i in range(groups - 1)])

    def spread(f):
        shaped = f.reshape(hl, 1, memories, 1)
        wide = jnp.broadcast_to(shaped, (hl, 1, memories, state.shape[1]))
        return wide.reshape(hl, 1, state.shape[2])

    held = state.astype(F32)
    step = 1
    while step < groups - 1:
        pairs = [(i, i + step) for i in range(groups - step)]
        earlier = lax.ppermute(held.astype(BF16), "hi", pairs).astype(F32)
        earlier_factor = lax.ppermute(factor, "hi", pairs)
        held = held + spread(factor) * earlier
        factor = factor * earlier_factor
        step *= 2
    return held.astype(BF16)


def shards(queries, keys, values, log_decay, routes, route_weight, gain):
    td, heads, hd = queries.shape[1:]
    memories = lax.axis_size("mem")
    lo = lax.axis_size("lo")
    groups = lax.axis_size("hi")
    g = memories * lo
    hl = heads // g
    axes = ("lo", "mem")
    kv_send, q_send = pack(
        queries[0], keys[0], values[0], log_decay[0].T, routes[0].T, route_weight[0].T, g, hl
    )
    kv = lax.all_to_all(kv_send, axes, split_axis=0, concat_axis=0, tiled=True)
    q = lax.all_to_all(q_send, axes, split_axis=0, concat_axis=0, tiled=True)
    state, total = local_state(kv, hl, memories, td)
    entering = entering_state(state, total, groups, hl, memories)
    place = lax.axis_index("lo") * memories + lax.axis_index("mem")
    own_gain = lax.dynamic_slice_in_dim(gain.reshape(heads, hd), place * hl, hl, 0)
    out = readout(q, kv, entering, own_gain, hl, memories, td)
    back = lax.all_to_all(out, axes, split_axis=0, concat_axis=0, tiled=True)
    return back.reshape(heads, td, hd).transpose(1, 0, 2)[None]


def solution(mesh):
    memories, blocks = mesh.shape["mem"], mesh.shape["ctx"]
    def call(queries, keys, values, log_decay, routes, route_weight, gain):
        heads = queries.shape[2]
        lo = max(
            s
            for s in range(1, max(1, blocks // 2) + 1)
            if blocks % s == 0 and heads % (memories * s) == 0
        )
        split = Mesh(mesh.devices.reshape(memories, blocks // lo, lo), ("mem", "hi", "lo"))
        tokens = P(("hi", "lo"), "mem")
        return jax.shard_map(
            shards,
            mesh=split,
            in_specs=(tokens,) * 6 + (P(),),
            out_specs=tokens,
            check_vma=False,
        )(queries, keys, values, log_decay, routes, route_weight, gain)

    return call
```

```python
import functools
import math

import jax
import jax.numpy as jnp
from jax import lax
from jax.experimental import pallas as pl
from jax.experimental.pallas import tpu as pltpu
from jax.sharding import Mesh
from jax.sharding import PartitionSpec as P

F32 = jnp.float32
BF16 = jnp.bfloat16
META = 16
ROWS = 8


def dot(a, b, dims=((1,), (0,))):
    return lax.dot_general(a, b, (dims, ((), ())), preferred_element_type=F32)


def split_heads(src, out, scr, hl, base, turned):
    td, hb, hd = src.shape
    scr[...] = src[...].astype(F32).reshape(td * hb, hd)
    for j in range(hb):
        start = base + (j % hl) * td
        rows = scr[pl.ds(j, td, stride=hb), :].astype(BF16)
        out[j // hl, start : start + td, :] = rows.T if turned else rows


def pack_kv_kernel(hl, k_ref, v_ref, ld_ref, rt_ref, wt_ref, out, scr_k, scr_v, ld_scr):
    i = pl.program_id(0)
    td, hb, _ = k_ref.shape

    @pl.when(i == 0)
    def _():
        ld_scr[...] = ld_ref[...].astype(F32)

    split_heads(k_ref, out, scr_k, hl, 0, False)
    split_heads(v_ref, out, scr_v, hl, hl * td, True)
    w = wt_ref[...]
    hi = w.astype(BF16).astype(F32)
    mid = (w - hi).astype(BF16).astype(F32)
    low = (w - hi) - mid
    table = jnp.concatenate([rt_ref[...].astype(F32), hi, mid, low], axis=0)
    here = ld_scr[pl.ds(pl.multiple_of(i * hb, hb), hb), :]
    for dd in range(hb // hl):
        own = (here if dd == 0 else pltpu.roll(here, hb - dd * hl, 0))[: META - ROWS]
        out[dd, 2 * hl * td :, :] = jnp.concatenate([table, own], axis=0).astype(BF16)


def pack_q_kernel(hl, q_ref, out, scr):
    split_heads(q_ref, out, scr, hl, 0, True)


def pack_kv(keys, values, ld_t, routes_t, weight_t, g, hl):
    td, heads, hd = keys.shape
    hb = math.gcd(heads, 16)
    rows = 2 * hl * td + META
    whole = lambda a: pl.BlockSpec(a.shape, lambda i: (0,) * a.ndim)
    block = pl.BlockSpec((td, hb, hd), lambda i: (0, i, 0))
    return pl.pallas_call(
        functools.partial(pack_kv_kernel, hl),
        grid=(heads // hb,),
        in_specs=[block, block, whole(ld_t), whole(routes_t), whole(weight_t)],
        out_specs=pl.BlockSpec((hb // hl, rows, hd), lambda i: (i, 0, 0)),
        out_shape=jax.ShapeDtypeStruct((g, rows, hd), BF16),
        scratch_shapes=[pltpu.VMEM((td * hb, hd), F32)] * 2 + [pltpu.VMEM((heads, td), F32)],
        name="pack_kv",
    )(keys, values, ld_t, routes_t, weight_t)


def pack_q(queries, g, hl):
    td, heads, hd = queries.shape
    hb = math.gcd(heads, 16)
    return pl.pallas_call(
        functools.partial(pack_q_kernel, hl),
        grid=(heads // hb,),
        in_specs=[pl.BlockSpec((td, hb, hd), lambda i: (0, i, 0))],
        out_specs=pl.BlockSpec((hb // hl, hl * td, hd), lambda i: (i, 0, 0)),
        out_shape=jax.ShapeDtypeStruct((g, hl * td, hd), BF16),
        scratch_shapes=[pltpu.VMEM((td * hb, hd), F32)],
        name="pack_q",
    )(queries)


def meta_rows(meta_ref, s, hl, memories):
    meta = meta_ref[s].astype(F32)
    td = meta.shape[1]
    row = lax.broadcasted_iota(jnp.int32, (ROWS, td), 0)
    memory = lax.rem(row, memories).astype(F32)
    first = meta[0:1] == memory
    second = meta[1:2] == memory
    rate = jnp.broadcast_to(meta[8:9], (ROWS, td))
    for h in range(1, hl):
        rate = jnp.where(row >= h * memories, meta[8 + h : 9 + h], rate)
    member = first | second
    return meta, first, second, member, jnp.where(member, rate, 0.0)


def running_sums(meta_ref, a_scr, cs_scr, g, hl, memories):
    td = a_scr.shape[1]
    for s in range(g):
        a_scr[s * ROWS : (s + 1) * ROWS, :] = meta_rows(meta_ref, s, hl, memories)[4]
    t0 = lax.broadcasted_iota(jnp.int32, (td, 2 * td), 0)
    t1 = lax.broadcasted_iota(jnp.int32, (td, 2 * td), 1)
    upper = jnp.where(t0 <= t1, 1.0, 0.0).astype(BF16)
    cs_scr[...] = dot(a_scr[...].astype(BF16), upper)


def state_kernel(
    g, hl, memories, td, meta_ref, kv_ref, state_ref, total_ref, a_scr, cs_scr, dec_scr, acc_scr
):
    i = pl.program_id(0)
    step = kv_ref.shape[0]
    hd = kv_ref.shape[2]

    @pl.when(i == 0)
    def _():
        running_sums(meta_ref, a_scr, cs_scr, g, hl, memories)
        after = jnp.zeros((ROWS, td), F32)
        for s in reversed(range(g)):
            member = meta_rows(meta_ref, s, hl, memories)[3]
            rows = slice(s * ROWS, (s + 1) * ROWS)
            running, total = cs_scr[rows, :td], cs_scr[rows, td:]
            dec_scr[s // step, :, s % step * td : (s % step + 1) * td] = jnp.where(
                member, jnp.exp(total - running + after), 0.0
            )
            after = after + total
        total_ref[...] = jnp.exp(after)
        acc_scr[...] = jnp.zeros_like(acc_scr)

    decay = dec_scr[i]
    for h in range(hl):
        key = jnp.concatenate([kv_ref[n, h * td : (h + 1) * td, :] for n in range(step)], axis=0)
        value = jnp.concatenate(
            [kv_ref[n, (hl + h) * td : (hl + h + 1) * td, :] for n in range(step)], axis=1
        ).astype(F32)
        for m in range(memories):
            j = h * memories + m
            acc_scr[h, m * hd : (m + 1) * hd, :] += dot((value * decay[j : j + 1, :]).astype(BF16), key)

    @pl.when(i == pl.num_programs(0) - 1)
    def _():
        state_ref[...] = acc_scr[...].astype(BF16)


def chunk_specs(kv, hl, td, step):
    g, rows, hd = kv.shape
    meta = pl.BlockSpec((g, META, hd), lambda i: (0, 2 * hl * td // META, 0))
    tokens = pl.BlockSpec((step, 2 * hl * td, hd), lambda i: (i, 0, 0))
    return [meta, tokens]


def local_state(kv, hl, memories, td):
    g, rows, hd = kv.shape
    step = math.gcd(g, 8)
    return pl.pallas_call(
        functools.partial(state_kernel, g, hl, memories, td),
        grid=(g // step,),
        in_specs=chunk_specs(kv, hl, td, step),
        out_specs=[
            pl.BlockSpec((hl, memories * hd, hd), lambda i: (0, 0, 0)),
            pl.BlockSpec((ROWS, td), lambda i: (0, 0)),
        ],
        out_shape=[
            jax.ShapeDtypeStruct((hl, memories * hd, hd), BF16),
            jax.ShapeDtypeStruct((ROWS, td), F32),
        ],
        scratch_shapes=[
            pltpu.VMEM((g * ROWS, td), F32),
            pltpu.VMEM((g * ROWS, 2 * td), F32),
            pltpu.VMEM((g // step, ROWS, step * td), F32),
            pltpu.VMEM((hl, memories * hd, hd), F32),
        ],
        cost_estimate=pl.CostEstimate(
            flops=2 * g * td * hl * memories * hd * hd, bytes_accessed=kv.size * 2, transcendentals=0
        ),
        name="local_state",
    )(kv, kv)


def chunk_kernel(
    g, hl, memories, td, meta_ref, kv_ref, lhs_ref, fac_ref, a_scr, cs_scr, col_scr, own_scr, st_scr
):
    i = pl.program_id(0)
    step = kv_ref.shape[0]
    hd = kv_ref.shape[2]
    scale = hd ** (-0.5)

    @pl.when(i == 0)
    def _():
        running_sums(meta_ref, a_scr, cs_scr, g, hl, memories)
        before = jnp.zeros((ROWS, td), F32)
        for s in range(g):
            meta, first, second, member, _ = meta_rows(meta_ref, s, hl, memories)
            rows = slice(s * ROWS, (s + 1) * ROWS)
            running, total = cs_scr[rows, :td], cs_scr[rows, td:]
            half = 0.5 * total
            weight = [meta[2 + n : 3 + n] + (meta[4 + n : 5 + n] + meta[6 + n : 7 + n]) for n in range(2)]
            col_scr[s] = jnp.where(member, jnp.exp(half - running), 0.0)
            own_scr[s] = jnp.exp(half)
            fac_ref[s, 0:ROWS, :] = jnp.exp(running - half) * scale
            fac_ref[s, ROWS : 2 * ROWS, :] = jnp.where(first, weight[0], 0.0) + jnp.where(
                second, weight[1], 0.0
            )
            fac_ref[s, 2 * ROWS :, :] = jnp.exp(before + half)
            before = before + total
        st_scr[...] = jnp.zeros_like(st_scr)

    for n in range(step):
        decay = col_scr[i * step + n]
        own = own_scr[i * step + n]
        for h in range(hl):
            key = kv_ref[n, h * td : (h + 1) * td, :]
            value = kv_ref[n, (hl + h) * td : (hl + h + 1) * td, :].astype(F32)
            for m in range(memories):
                j = h * memories + m
                rows = slice(m * hd, (m + 1) * hd)
                scaled = (value * decay[j : j + 1, :]).astype(BF16)
                lhs_ref[n, h, rows, :td] = scaled
                grown = dot(scaled, key)
                state = st_scr[h, rows, :] * own[j : j + 1, :]
                lhs_ref[n, h, rows, td:] = state.astype(BF16)
                st_scr[h, rows, :] = (state + grown) * own[j : j + 1, :]


def chunk_states(kv, hl, memories, td):
    g, rows, hd = kv.shape
    step = math.gcd(g, 8)
    return pl.pallas_call(
        functools.partial(chunk_kernel, g, hl, memories, td),
        grid=(g // step,),
        in_specs=chunk_specs(kv, hl, td, step),
        out_specs=[
            pl.BlockSpec((step, hl, memories * hd, td + hd), lambda i: (i, 0, 0, 0)),
            pl.BlockSpec((g, 3 * ROWS, td), lambda i: (0, 0, 0)),
        ],
        out_shape=[
            jax.ShapeDtypeStruct((g, hl, memories * hd, td + hd), BF16),
            jax.ShapeDtypeStruct((g, 3 * ROWS, td), F32),
        ],
        scratch_shapes=[
            pltpu.VMEM((g * ROWS, td), F32),
            pltpu.VMEM((g * ROWS, 2 * td), F32),
            pltpu.VMEM((g, ROWS, td), F32),
            pltpu.VMEM((g, ROWS, td), F32),
            pltpu.VMEM((hl, memories * hd, hd), F32),
        ],
        cost_estimate=pl.CostEstimate(
            flops=2 * g * td * hl * memories * hd * hd, bytes_accessed=kv.size * 10, transcendentals=0
        ),
        name="chunk_states",
    )(kv, kv)


def readout_kernel(
    hl, memories, td, q_ref, k_ref, lhs_ref, fac_ref, state_ref, gain_ref, out_ref, st_scr, gain_scr, acc_scr
):
    hd = q_ref.shape[2]

    @pl.when(pl.program_id(0) == 0)
    def _():
        st_scr[...] = state_ref[...].astype(F32)
        for h in range(hl):
            gain_scr[h] = jnp.broadcast_to(gain_ref[h : h + 1, :], (td, hd)).T

    causal = lax.broadcasted_iota(jnp.int32, (td, td), 0) <= lax.broadcasted_iota(jnp.int32, (td, td), 1)
    units = [(c, h) for c in range(q_ref.shape[0]) for h in range(hl)]
    right = []
    for c, h in units:
        query = q_ref[c, h * td : (h + 1) * td, :]
        key = k_ref[c, h * td : (h + 1) * td, :]
        scores = jnp.where(causal, dot(key, query), 0.0).astype(BF16)
        right.append(jnp.concatenate([scores, query], axis=0))
    for u, (c, h) in enumerate(units):
        for m in range(memories):
            j = 2 * ROWS + h * memories + m
            rows = slice(m * hd, (m + 1) * hd)
            state = lhs_ref[c, h, rows, td:].astype(F32) + st_scr[h, rows, :] * fac_ref[c, j : j + 1, :]
            left = jnp.concatenate([lhs_ref[c, h, rows, :td], state.astype(BF16)], axis=1)
            acc_scr[u, rows, :] = dot(left, right[u])
    for u, (c, h) in enumerate(units):
        mixed = jnp.zeros((hd, td), F32)
        for m in range(memories):
            j = h * memories + m
            read = acc_scr[u, m * hd : (m + 1) * hd, :] * fac_ref[c, j : j + 1, :]
            mean = jnp.sum(read * read, axis=0, keepdims=True) * (1.0 / hd)
            mixed = mixed + read * (lax.rsqrt(mean + 1e-06) * fac_ref[c, ROWS + j : ROWS + j + 1, :])
        out_ref[c, h * td : (h + 1) * td, :] = (mixed * gain_scr[h]).astype(BF16).T


def readout(q, kv, lhs, factors, state, gain, hl, memories, td):
    g, rows, hd = q.shape
    step = math.gcd(g, 8)
    tokens = pl.BlockSpec((step, hl * td, hd), lambda i: (i, 0, 0))
    return pl.pallas_call(
        functools.partial(readout_kernel, hl, memories, td),
        grid=(g // step,),
        in_specs=[
            tokens,
            tokens,
            pl.BlockSpec((step,) + lhs.shape[1:], lambda i: (i, 0, 0, 0)),
            pl.BlockSpec((step,) + factors.shape[1:], lambda i: (i, 0, 0)),
            pl.BlockSpec(state.shape, lambda i: (0, 0, 0)),
            pl.BlockSpec(gain.shape, lambda i: (0, 0)),
        ],
        out_specs=tokens,
        out_shape=jax.ShapeDtypeStruct(q.shape, BF16),
        scratch_shapes=[
            pltpu.VMEM(state.shape, F32),
            pltpu.VMEM((hl, hd, td), F32),
            pltpu.VMEM((step * hl, memories * hd, td), F32),
        ],
        cost_estimate=pl.CostEstimate(
            flops=8 * g * td * hl * memories * hd * hd, bytes_accessed=kv.size * 10, transcendentals=0
        ),
        name="readout",
    )(q, kv, lhs, factors, state, gain)


def entering_state(state, total, groups, hl, memories):
    if groups == 1:
        return jnp.zeros_like(state)
    state = lax.ppermute(state, "hi", [(i, i + 1) for i in range(groups - 1)])
    if groups == 2:
        return state
    factor = lax.ppermute(total[:, :1], "hi", [(i, i + 1) for i in range(groups - 1)])

    def spread(f):
        wide = jnp.broadcast_to(f.reshape(hl, memories, 1), (hl, memories, state.shape[2]))
        return wide.reshape(hl, state.shape[1], 1)

    held = state.astype(F32)
    step = 1
    while step < groups - 1:
        pairs = [(i, i + step) for i in range(groups - step)]
        earlier = lax.ppermute(held.astype(BF16), "hi", pairs).astype(F32)
        earlier_factor = lax.ppermute(factor, "hi", pairs)
        held = held + spread(factor) * earlier
        factor = factor * earlier_factor
        step *= 2
    return held.astype(BF16)


def shards(queries, keys, values, log_decay, routes, route_weight, gain):
    td, heads, hd = queries.shape[1:]
    memories = lax.axis_size("mem")
    lo = lax.axis_size("lo")
    groups = lax.axis_size("hi")
    g = memories * lo
    hl = heads // g
    axes = ("lo", "mem")
    kv_send = pack_kv(
        keys[0], values[0], log_decay[0].T, routes[0].T, route_weight[0].T, g, hl
    )
    q_send = pack_q(queries[0], g, hl)
    kv = lax.all_to_all(kv_send, axes, split_axis=0, concat_axis=0, tiled=True)
    q = lax.all_to_all(q_send, axes, split_axis=0, concat_axis=0, tiled=True)
    state, total = local_state(kv, hl, memories, td)
    entering = entering_state(state, total, groups, hl, memories)
    place = lax.axis_index("lo") * memories + lax.axis_index("mem")
    own_gain = lax.dynamic_slice_in_dim(gain.reshape(heads, hd), place * hl, hl, 0)
    lhs, factors = chunk_states(kv, hl, memories, td)
    out = readout(q, kv, lhs, factors, entering, own_gain, hl, memories, td)
    back = lax.all_to_all(out, axes, split_axis=0, concat_axis=0, tiled=True)
    return back.reshape(heads, td, hd).transpose(1, 0, 2)[None]


def solution(mesh):
    memories, blocks = mesh.shape["mem"], mesh.shape["ctx"]
    def call(queries, keys, values, log_decay, routes, route_weight, gain):
        heads = queries.shape[2]
        lo = max(
            s
            for s in range(1, max(1, blocks // 2) + 1)
            if blocks % s == 0 and heads % (memories * s) == 0
        )
        split = Mesh(mesh.devices.reshape(memories, blocks // lo, lo), ("mem", "hi", "lo"))
        tokens = P(("hi", "lo"), "mem")
        return jax.shard_map(
            shards,
            mesh=split,
            in_specs=(tokens,) * 6 + (P(),),
            out_specs=tokens,
            check_vma=False,
        )(queries, keys, values, log_decay, routes, route_weight, gain)

    return call
```

```python
import functools
import math

import jax
import jax.numpy as jnp
from jax import lax
from jax.experimental import pallas as pl
from jax.experimental.pallas import tpu as pltpu
from jax.sharding import Mesh
from jax.sharding import PartitionSpec as P

F32 = jnp.float32
BF16 = jnp.bfloat16
META = 16
PARAMS = pltpu.CompilerParams(vmem_limit_bytes=50 << 20)
ROWS = 8


def dot(a, b, dims=((1,), (0,))):
    return lax.dot_general(a, b, (dims, ((), ())), preferred_element_type=F32)


def split_heads(src, place, scr, hl, base, turned):
    td, hb, hd = src.shape
    scr[...] = src[...].astype(F32).reshape(td * hb, hd)
    for j in range(hb):
        start = base + (j % hl) * td
        rows = scr[pl.ds(j, td, stride=hb), :].astype(BF16)
        place(j // hl)[start : start + td, :] = rows.T if turned else rows


def pack_kv_kernel(hl, lo, k_ref, v_ref, ld_ref, rt_ref, wt_ref, out, scr_k, scr_v, ld_scr):
    i = pl.program_id(0)
    td, hb, _ = k_ref.shape
    place = lambda dd: out.at[dd % lo, dd // lo]

    @pl.when(i == 0)
    def _():
        ld_scr[...] = ld_ref[...].astype(F32)

    split_heads(k_ref, place, scr_k, hl, 0, False)
    split_heads(v_ref, place, scr_v, hl, hl * td, True)
    w = wt_ref[...]
    hi = w.astype(BF16).astype(F32)
    mid = (w - hi).astype(BF16).astype(F32)
    low = (w - hi) - mid
    table = jnp.concatenate([rt_ref[...].astype(F32), hi, mid, low], axis=0)
    here = ld_scr[pl.ds(pl.multiple_of(i * hb, hb), hb), :]
    for dd in range(hb // hl):
        own = (here if dd == 0 else pltpu.roll(here, hb - dd * hl, 0))[: META - ROWS]
        place(dd)[2 * hl * td :, :] = jnp.concatenate([table, own], axis=0).astype(BF16)


def pack_q_kernel(hl, q_ref, out, scr):
    split_heads(q_ref, lambda dd: out.at[dd], scr, hl, 0, True)


def pack_kv(keys, values, ld_t, routes_t, weight_t, lo, memories, hl):
    td, heads, hd = keys.shape
    hb = math.gcd(heads, 16)
    rows = 2 * hl * td + META
    whole = lambda a: pl.BlockSpec(a.shape, lambda i: (0,) * a.ndim)
    block = pl.BlockSpec((td, hb, hd), lambda i: (0, i, 0))
    return pl.pallas_call(
        functools.partial(pack_kv_kernel, hl, lo),
        grid=(heads // hb,),
        in_specs=[block, block, whole(ld_t), whole(routes_t), whole(weight_t)],
        out_specs=pl.BlockSpec((lo, hb // hl // lo, rows, hd), lambda i: (0, i, 0, 0)),
        out_shape=jax.ShapeDtypeStruct((lo, memories, rows, hd), BF16),
        scratch_shapes=[pltpu.VMEM((td * hb, hd), F32)] * 2 + [pltpu.VMEM((heads, td), F32)],
        name="pack_kv",
    )(keys, values, ld_t, routes_t, weight_t)


def pack_q(queries, g, hl):
    td, heads, hd = queries.shape
    hb = math.gcd(heads, 16)
    return pl.pallas_call(
        functools.partial(pack_q_kernel, hl),
        grid=(heads // hb,),
        in_specs=[pl.BlockSpec((td, hb, hd), lambda i: (0, i, 0))],
        out_specs=pl.BlockSpec((hb // hl, hl * td, hd), lambda i: (i, 0, 0)),
        out_shape=jax.ShapeDtypeStruct((g, hl * td, hd), BF16),
        scratch_shapes=[pltpu.VMEM((td * hb, hd), F32)],
        name="pack_q",
    )(queries)


def meta_rows(meta_ref, s, hl, memories):
    meta = meta_ref[s].astype(F32)
    td = meta.shape[1]
    row = lax.broadcasted_iota(jnp.int32, (ROWS, td), 0)
    memory = lax.rem(row, memories).astype(F32)
    first = meta[0:1] == memory
    second = meta[1:2] == memory
    rate = jnp.broadcast_to(meta[8:9], (ROWS, td))
    for h in range(1, hl):
        rate = jnp.where(row >= h * memories, meta[8 + h : 9 + h], rate)
    member = first | second
    return meta, first, second, member, jnp.where(member, rate, 0.0)


def running_sums(meta_ref, a_scr, cs_scr, g, hl, memories):
    td = a_scr.shape[1]
    for s in range(g):
        a_scr[s * ROWS : (s + 1) * ROWS, :] = meta_rows(meta_ref, s, hl, memories)[4]
    t0 = lax.broadcasted_iota(jnp.int32, (td, 2 * td), 0)
    t1 = lax.broadcasted_iota(jnp.int32, (td, 2 * td), 1)
    upper = jnp.where(t0 <= t1, 1.0, 0.0).astype(BF16)
    cs_scr[...] = dot(a_scr[...].astype(BF16), upper)


def state_kernel(
    g, hl, memories, td, meta_ref, kv_ref, state_ref, total_ref, a_scr, cs_scr, dec_scr, acc_scr
):
    i = pl.program_id(0)
    step = kv_ref.shape[0]
    hd = kv_ref.shape[2]

    @pl.when(i == 0)
    def _():
        running_sums(meta_ref, a_scr, cs_scr, g, hl, memories)
        after = jnp.zeros((ROWS, td), F32)
        for s in reversed(range(g)):
            member = meta_rows(meta_ref, s, hl, memories)[3]
            rows = slice(s * ROWS, (s + 1) * ROWS)
            running, total = cs_scr[rows, :td], cs_scr[rows, td:]
            dec_scr[s // step, :, s % step * td : (s % step + 1) * td] = jnp.where(
                member, jnp.exp(total - running + after), 0.0
            )
            after = after + total
        total_ref[...] = jnp.exp(after)
        acc_scr[...] = jnp.zeros_like(acc_scr)

    decay = dec_scr[i]
    for h in range(hl):
        key = jnp.concatenate([kv_ref[n, h * td : (h + 1) * td, :] for n in range(step)], axis=0)
        value = jnp.concatenate(
            [kv_ref[n, (hl + h) * td : (hl + h + 1) * td, :] for n in range(step)], axis=1
        ).astype(F32)
        for m in range(memories):
            j = h * memories + m
            acc_scr[h, m * hd : (m + 1) * hd, :] += dot((value * decay[j : j + 1, :]).astype(BF16), key)

    @pl.when(i == pl.num_programs(0) - 1)
    def _():
        state_ref[...] = acc_scr[...].astype(BF16)


def chunk_specs(kv, hl, td, step):
    g, rows, hd = kv.shape
    meta = pl.BlockSpec((g, META, hd), lambda i: (0, 2 * hl * td // META, 0))
    tokens = pl.BlockSpec((step, 2 * hl * td, hd), lambda i: (i, 0, 0))
    return [meta, tokens]


def local_state(kv, hl, memories, td):
    g, rows, hd = kv.shape
    step = math.gcd(g, 8)
    return pl.pallas_call(
        functools.partial(state_kernel, g, hl, memories, td),
        grid=(g // step,),
        in_specs=chunk_specs(kv, hl, td, step),
        out_specs=[
            pl.BlockSpec((hl, memories * hd, hd), lambda i: (0, 0, 0)),
            pl.BlockSpec((ROWS, td), lambda i: (0, 0)),
        ],
        out_shape=[
            jax.ShapeDtypeStruct((hl, memories * hd, hd), BF16),
            jax.ShapeDtypeStruct((ROWS, td), F32),
        ],
        scratch_shapes=[
            pltpu.VMEM((g * ROWS, td), F32),
            pltpu.VMEM((g * ROWS, 2 * td), F32),
            pltpu.VMEM((g // step, ROWS, step * td), F32),
            pltpu.VMEM((hl, memories * hd, hd), F32),
        ],
        compiler_params=PARAMS,
        cost_estimate=pl.CostEstimate(
            flops=2 * g * td * hl * memories * hd * hd, bytes_accessed=kv.size * 2, transcendentals=0
        ),
        name="local_state",
    )(kv, kv)


def factor_kernel(g, hl, memories, td, meta_ref, fac_ref, a_scr, cs_scr):
    scale = meta_ref.shape[2] ** (-0.5)
    running_sums(meta_ref, a_scr, cs_scr, g, hl, memories)
    before = jnp.zeros((ROWS, td), F32)
    for s in range(g):
        meta, first, second, member, _ = meta_rows(meta_ref, s, hl, memories)
        rows = slice(s * ROWS, (s + 1) * ROWS)
        running, total = cs_scr[rows, :td], cs_scr[rows, td:]
        half = 0.5 * total
        weight = [meta[2 + n : 3 + n] + (meta[4 + n : 5 + n] + meta[6 + n : 7 + n]) for n in range(2)]
        fac_ref[s, 0:ROWS, :] = jnp.exp(running - half) * scale
        fac_ref[s, ROWS : 2 * ROWS, :] = jnp.where(first, weight[0], 0.0) + jnp.where(
            second, weight[1], 0.0
        )
        fac_ref[s, 2 * ROWS : 3 * ROWS, :] = jnp.exp(before + half)
        fac_ref[s, 3 * ROWS : 4 * ROWS, :] = jnp.where(member, jnp.exp(half - running), 0.0)
        fac_ref[s, 4 * ROWS :, :] = jnp.exp(half)
        before = before + total


def chunk_factors(kv, hl, memories, td):
    g, rows, hd = kv.shape
    return pl.pallas_call(
        functools.partial(factor_kernel, g, hl, memories, td),
        grid=(1,),
        in_specs=chunk_specs(kv, hl, td, 1)[:1],
        out_specs=pl.BlockSpec((g, 5 * ROWS, td), lambda i: (0, 0, 0)),
        out_shape=jax.ShapeDtypeStruct((g, 5 * ROWS, td), F32),
        scratch_shapes=[pltpu.VMEM((g * ROWS, td), F32), pltpu.VMEM((g * ROWS, 2 * td), F32)],
        compiler_params=PARAMS,
        cost_estimate=pl.CostEstimate(flops=g * td * td, bytes_accessed=g * td * 200, transcendentals=0),
        name="chunk_factors",
    )(kv)


def chunk_kernel(hl, memories, td, fac_ref, kv_ref, lhs_ref, st_scr):
    hd = kv_ref.shape[2]

    @pl.when(pl.program_id(0) == 0)
    def _():
        st_scr[...] = jnp.zeros_like(st_scr)

    for n in range(kv_ref.shape[0]):
        for h in range(hl):
            key = kv_ref[n, h * td : (h + 1) * td, :]
            value = kv_ref[n, (hl + h) * td : (hl + h + 1) * td, :].astype(F32)
            for m in range(memories):
                j = h * memories + m
                rows = slice(m * hd, (m + 1) * hd)
                own = fac_ref[n, 4 * ROWS + j : 4 * ROWS + j + 1, :]
                scaled = (value * fac_ref[n, 3 * ROWS + j : 3 * ROWS + j + 1, :]).astype(BF16)
                lhs_ref[n, h, rows, :td] = scaled
                grown = dot(scaled, key)
                state = st_scr[h, rows, :] * own
                lhs_ref[n, h, rows, td:] = state.astype(BF16)
                st_scr[h, rows, :] = (state + grown) * own


def chunk_states(kv, factors, hl, memories, td):
    g, rows, hd = kv.shape
    step = math.gcd(g, 8)
    return pl.pallas_call(
        functools.partial(chunk_kernel, hl, memories, td),
        grid=(g // step,),
        in_specs=[
            pl.BlockSpec((step,) + factors.shape[1:], lambda i: (i, 0, 0)),
            chunk_specs(kv, hl, td, step)[1],
        ],
        out_specs=pl.BlockSpec((step, hl, memories * hd, td + hd), lambda i: (i, 0, 0, 0)),
        out_shape=jax.ShapeDtypeStruct((g, hl, memories * hd, td + hd), BF16),
        scratch_shapes=[pltpu.VMEM((hl, memories * hd, hd), F32)],
        compiler_params=PARAMS,
        cost_estimate=pl.CostEstimate(
            flops=2 * g * td * hl * memories * hd * hd, bytes_accessed=kv.size * 10, transcendentals=0
        ),
        name="chunk_states",
    )(factors, kv)


def readout_kernel(
    hl, memories, lo, td, q_ref, k_ref, lhs_ref, fac_ref, state_ref, gain_ref, out_ref,
    st_scr, gain_scr, acc_scr,
):
    hd = q_ref.shape[3]
    part = q_ref.shape[0]
    i = pl.program_id(0)

    @pl.when(i == 0)
    def _():
        st_scr[...] = state_ref[...].astype(F32)
        place = lax.axis_index("mem") * lo + lax.axis_index("lo")
        for h in range(hl):
            own = gain_ref[pl.ds(place * hl + h, 1), :]
            gain_scr[h] = jnp.broadcast_to(own, (td, hd)).T

    causal = lax.broadcasted_iota(jnp.int32, (td, td), 0) <= lax.broadcasted_iota(jnp.int32, (td, td), 1)
    units = [(a, b, h) for b in range(lo) for a in range(part) for h in range(hl)]
    right = []
    for a, b, h in units:
        query = q_ref[a, b, h * td : (h + 1) * td, :]
        key = k_ref[b, a, h * td : (h + 1) * td, :]
        scores = jnp.where(causal, dot(key, query), 0.0).astype(BF16)
        right.append(jnp.concatenate([scores, query], axis=0))
    for u, (a, b, h) in enumerate(units):
        s = b * memories + i * part + a
        for m in range(memories):
            j = 2 * ROWS + h * memories + m
            rows = slice(m * hd, (m + 1) * hd)
            state = lhs_ref[b, a, h, rows, td:].astype(F32) + st_scr[h, rows, :] * fac_ref[s, j : j + 1, :]
            left = jnp.concatenate([lhs_ref[b, a, h, rows, :td], state.astype(BF16)], axis=1)
            acc_scr[u, rows, :] = dot(left, right[u])
    for u, (a, b, h) in enumerate(units):
        s = b * memories + i * part + a
        mixed = None
        for m in range(memories):
            j = h * memories + m
            read = acc_scr[u, m * hd : (m + 1) * hd, :] * fac_ref[s, j : j + 1, :]
            mean = jnp.sum(read * read, axis=0, keepdims=True) * (1.0 / hd)
            term = read * (lax.rsqrt(mean + 1e-06) * fac_ref[s, ROWS + j : ROWS + j + 1, :])
            mixed = term if mixed is None else mixed + term
        out_ref[a, b, h * td : (h + 1) * td, :] = (mixed * gain_scr[h]).astype(BF16).T


def readout(q, kv, lhs, factors, state, gain, lo, hl, memories, td):
    g, _, hd = q.shape
    part = max(1, math.gcd(memories, 8 // math.gcd(lo, 8)))
    q = q.reshape(memories, lo, hl * td, hd)
    tokens = pl.BlockSpec((part, lo, hl * td, hd), lambda i: (i, 0, 0, 0))
    out = pl.pallas_call(
        functools.partial(readout_kernel, hl, memories, lo, td),
        grid=(memories // part,),
        in_specs=[
            tokens,
            pl.BlockSpec((lo, part, hl * td, hd), lambda i: (0, i, 0, 0)),
            pl.BlockSpec((lo, part) + lhs.shape[1:], lambda i: (0, i, 0, 0, 0)),
            pl.BlockSpec(factors.shape, lambda i: (0, 0, 0)),
            pl.BlockSpec(state.shape, lambda i: (0, 0, 0)),
            pl.BlockSpec(gain.shape, lambda i: (0, 0)),
        ],
        out_specs=tokens,
        out_shape=jax.ShapeDtypeStruct(q.shape, BF16),
        scratch_shapes=[
            pltpu.VMEM(state.shape, F32),
            pltpu.VMEM((hl, hd, td), F32),
            pltpu.VMEM((part * lo * hl, memories * hd, td), F32),
        ],
        compiler_params=PARAMS,
        cost_estimate=pl.CostEstimate(
            flops=8 * g * td * hl * memories * hd * hd, bytes_accessed=kv.size * 10, transcendentals=0
        ),
        name="readout",
    )(
        q,
        kv.reshape((lo, memories) + kv.shape[1:]),
        lhs.reshape((lo, memories) + lhs.shape[1:]),
        factors,
        state,
        gain,
    )
    return out.reshape(g, hl * td, hd)


def entering_state(state, total, groups, hl, memories):
    if groups == 1:
        return jnp.zeros_like(state)
    state = lax.ppermute(state, "hi", [(i, i + 1) for i in range(groups - 1)])
    if groups == 2:
        return state
    factor = lax.ppermute(total[:, :1], "hi", [(i, i + 1) for i in range(groups - 1)])

    def spread(f):
        wide = jnp.broadcast_to(f.reshape(hl, memories, 1), (hl, memories, state.shape[2]))
        return wide.reshape(hl, state.shape[1], 1)

    held = state.astype(F32)
    step = 1
    while step < groups - 1:
        pairs = [(i, i + step) for i in range(groups - step)]
        earlier = lax.ppermute(held.astype(BF16), "hi", pairs).astype(F32)
        earlier_factor = lax.ppermute(factor, "hi", pairs)
        held = held + spread(factor) * earlier
        factor = factor * earlier_factor
        step *= 2
    return held.astype(BF16)


def shards(queries, keys, values, log_decay, routes, route_weight, gain):
    td, heads, hd = queries.shape[1:]
    memories = lax.axis_size("mem")
    lo = lax.axis_size("lo")
    groups = lax.axis_size("hi")
    g = memories * lo
    hl = heads // g
    kv_send = pack_kv(
        keys[0], values[0], log_decay[0].T, routes[0].T, route_weight[0].T, lo, memories, hl
    ).reshape(g, 2 * hl * td + META, hd)
    q_send = pack_q(queries[0], g, hl)
    kv = lax.all_to_all(kv_send, ("lo", "mem"), split_axis=0, concat_axis=0, tiled=True)
    q = lax.all_to_all(q_send, ("mem", "lo"), split_axis=0, concat_axis=0, tiled=True)
    state, total = local_state(kv, hl, memories, td)
    entering = entering_state(state, total, groups, hl, memories)
    factors = chunk_factors(kv, hl, memories, td)
    lhs = chunk_states(kv, factors, hl, memories, td)
    out = readout(q, kv, lhs, factors, entering, gain.reshape(heads, hd), lo, hl, memories, td)
    back = lax.all_to_all(out, ("mem", "lo"), split_axis=0, concat_axis=0, tiled=True)
    return back.reshape(heads, td, hd).transpose(1, 0, 2)[None]


def solution(mesh):
    memories, blocks = mesh.shape["mem"], mesh.shape["ctx"]
    def call(queries, keys, values, log_decay, routes, route_weight, gain):
        heads = queries.shape[2]
        lo = max(
            s
            for s in range(1, max(1, blocks // 2) + 1)
            if blocks % s == 0 and heads % (memories * s) == 0
        )
        split = Mesh(mesh.devices.reshape(memories, blocks // lo, lo), ("mem", "hi", "lo"))
        tokens = P(("hi", "lo"), "mem")
        return jax.shard_map(
            shards,
            mesh=split,
            in_specs=(tokens,) * 6 + (P(),),
            out_specs=tokens,
            check_vma=False,
        )(queries, keys, values, log_decay, routes, route_weight, gain)

    return call
```

```python
import functools
import math

import jax
import jax.numpy as jnp
from jax import lax
from jax.experimental import pallas as pl
from jax.experimental.pallas import tpu as pltpu
from jax.sharding import Mesh
from jax.sharding import PartitionSpec as P

F32 = jnp.float32
BF16 = jnp.bfloat16
META = 16
PARAMS = pltpu.CompilerParams(vmem_limit_bytes=50 << 20)
ROWS = 8


def dot(a, b, dims=((1,), (0,))):
    return lax.dot_general(a, b, (dims, ((), ())), preferred_element_type=F32)


def split_heads(src, place, scr, hl, base, turned):
    td, hb, hd = src.shape
    scr[...] = src[...].astype(F32).reshape(td * hb, hd)
    for j in range(hb):
        start = base + (j % hl) * td
        rows = scr[pl.ds(j, td, stride=hb), :].astype(BF16)
        place(j // hl)[start : start + td, :] = rows.T if turned else rows


def pack_kernel(hl, lo, k_ref, v_ref, q_ref, ld_ref, rt_ref, wt_ref, out, q_out, scr_k, scr_v, scr_q, ld_scr):
    i = pl.program_id(0)
    td, hb, _ = k_ref.shape
    place = lambda dd: out.at[dd % lo, dd // lo]

    @pl.when(i == 0)
    def _():
        ld_scr[...] = ld_ref[...].astype(F32)

    split_heads(k_ref, place, scr_k, hl, 0, False)
    split_heads(v_ref, place, scr_v, hl, hl * td, True)
    split_heads(q_ref, lambda dd: q_out.at[dd], scr_q, hl, 0, True)
    w = wt_ref[...]
    hi = w.astype(BF16).astype(F32)
    mid = (w - hi).astype(BF16).astype(F32)
    low = (w - hi) - mid
    table = jnp.concatenate([rt_ref[...].astype(F32), hi, mid, low], axis=0)
    here = ld_scr[pl.ds(pl.multiple_of(i * hb, hb), hb), :]
    for dd in range(hb // hl):
        own = (here if dd == 0 else pltpu.roll(here, hb - dd * hl, 0))[: META - ROWS]
        place(dd)[2 * hl * td :, :] = jnp.concatenate([table, own], axis=0).astype(BF16)


def pack(keys, values, queries, ld_t, routes_t, weight_t, lo, memories, hl):
    td, heads, hd = keys.shape
    hb = math.gcd(heads, 16)
    rows = 2 * hl * td + META
    whole = lambda a: pl.BlockSpec(a.shape, lambda i: (0,) * a.ndim)
    block = pl.BlockSpec((td, hb, hd), lambda i: (0, i, 0))
    return pl.pallas_call(
        functools.partial(pack_kernel, hl, lo),
        grid=(heads // hb,),
        in_specs=[block, block, block, whole(ld_t), whole(routes_t), whole(weight_t)],
        out_specs=[
            pl.BlockSpec((lo, hb // hl // lo, rows, hd), lambda i: (0, i, 0, 0)),
            pl.BlockSpec((hb // hl, hl * td, hd), lambda i: (i, 0, 0)),
        ],
        out_shape=[
            jax.ShapeDtypeStruct((lo, memories, rows, hd), BF16),
            jax.ShapeDtypeStruct((lo * memories, hl * td, hd), BF16),
        ],
        scratch_shapes=[pltpu.VMEM((td * hb, hd), F32)] * 3 + [pltpu.VMEM((heads, td), F32)],
        name="pack",
    )(keys, values, queries, ld_t, routes_t, weight_t)


def meta_rows(meta_ref, s, hl, memories):
    meta = meta_ref[s].astype(F32)
    td = meta.shape[1]
    row = lax.broadcasted_iota(jnp.int32, (ROWS, td), 0)
    memory = lax.rem(row, memories).astype(F32)
    first = meta[0:1] == memory
    second = meta[1:2] == memory
    rate = jnp.broadcast_to(meta[8:9], (ROWS, td))
    for h in range(1, hl):
        rate = jnp.where(row >= h * memories, meta[8 + h : 9 + h], rate)
    member = first | second
    return meta, first, second, member, jnp.where(member, rate, 0.0)


def running_sums(meta_ref, a_scr, cs_scr, g, hl, memories):
    td = a_scr.shape[1]
    for s in range(g):
        a_scr[s * ROWS : (s + 1) * ROWS, :] = meta_rows(meta_ref, s, hl, memories)[4]
    t0 = lax.broadcasted_iota(jnp.int32, (td, 2 * td), 0)
    t1 = lax.broadcasted_iota(jnp.int32, (td, 2 * td), 1)
    upper = jnp.where(t0 <= t1, 1.0, 0.0).astype(BF16)
    cs_scr[...] = dot(a_scr[...].astype(BF16), upper)


def state_kernel(
    g, hl, memories, td, meta_ref, kv_ref, state_ref, total_ref, a_scr, cs_scr, dec_scr, acc_scr
):
    i = pl.program_id(0)
    step = kv_ref.shape[0]
    hd = kv_ref.shape[2]

    @pl.when(i == 0)
    def _():
        running_sums(meta_ref, a_scr, cs_scr, g, hl, memories)
        after = jnp.zeros((ROWS, td), F32)
        for s in reversed(range(g)):
            member = meta_rows(meta_ref, s, hl, memories)[3]
            rows = slice(s * ROWS, (s + 1) * ROWS)
            running, total = cs_scr[rows, :td], cs_scr[rows, td:]
            dec_scr[s // step, :, s % step * td : (s % step + 1) * td] = jnp.where(
                member, jnp.exp(total - running + after), 0.0
            )
            after = after + total
        total_ref[...] = jnp.exp(after)
        acc_scr[...] = jnp.zeros_like(acc_scr)

    decay = dec_scr[i]
    for h in range(hl):
        key = jnp.concatenate([kv_ref[n, h * td : (h + 1) * td, :] for n in range(step)], axis=0)
        value = jnp.concatenate(
            [kv_ref[n, (hl + h) * td : (hl + h + 1) * td, :] for n in range(step)], axis=1
        ).astype(F32)
        for m in range(memories):
            j = h * memories + m
            acc_scr[h, m * hd : (m + 1) * hd, :] += dot((value * decay[j : j + 1, :]).astype(BF16), key)

    @pl.when(i == pl.num_programs(0) - 1)
    def _():
        state_ref[...] = acc_scr[...].astype(BF16)


def chunk_specs(kv, hl, td, step):
    g, rows, hd = kv.shape
    meta = pl.BlockSpec((g, META, hd), lambda i: (0, 2 * hl * td // META, 0))
    tokens = pl.BlockSpec((step, 2 * hl * td, hd), lambda i: (i, 0, 0))
    return [meta, tokens]


def local_state(kv, hl, memories, td):
    g, rows, hd = kv.shape
    step = math.gcd(g, 8)
    return pl.pallas_call(
        functools.partial(state_kernel, g, hl, memories, td),
        grid=(g // step,),
        in_specs=chunk_specs(kv, hl, td, step),
        out_specs=[
            pl.BlockSpec((hl, memories * hd, hd), lambda i: (0, 0, 0)),
            pl.BlockSpec((ROWS, td), lambda i: (0, 0)),
        ],
        out_shape=[
            jax.ShapeDtypeStruct((hl, memories * hd, hd), BF16),
            jax.ShapeDtypeStruct((ROWS, td), F32),
        ],
        scratch_shapes=[
            pltpu.VMEM((g * ROWS, td), F32),
            pltpu.VMEM((g * ROWS, 2 * td), F32),
            pltpu.VMEM((g // step, ROWS, step * td), F32),
            pltpu.VMEM((hl, memories * hd, hd), F32),
        ],
        compiler_params=PARAMS,
        cost_estimate=pl.CostEstimate(
            flops=2 * g * td * hl * memories * hd * hd, bytes_accessed=kv.size * 2, transcendentals=0
        ),
        name="local_state",
    )(kv, kv)


def factor_kernel(g, hl, memories, td, meta_ref, fac_ref, a_scr, cs_scr):
    scale = meta_ref.shape[2] ** (-0.5)
    running_sums(meta_ref, a_scr, cs_scr, g, hl, memories)
    before = jnp.zeros((ROWS, td), F32)
    for s in range(g):
        meta, first, second, member, _ = meta_rows(meta_ref, s, hl, memories)
        rows = slice(s * ROWS, (s + 1) * ROWS)
        running, total = cs_scr[rows, :td], cs_scr[rows, td:]
        half = 0.5 * total
        weight = [meta[2 + n : 3 + n] + (meta[4 + n : 5 + n] + meta[6 + n : 7 + n]) for n in range(2)]
        fac_ref[s, 0:ROWS, :] = jnp.exp(running - half) * scale
        fac_ref[s, ROWS : 2 * ROWS, :] = jnp.where(first, weight[0], 0.0) + jnp.where(
            second, weight[1], 0.0
        )
        fac_ref[s, 2 * ROWS : 3 * ROWS, :] = jnp.exp(before + half)
        fac_ref[s, 3 * ROWS : 4 * ROWS, :] = jnp.where(member, jnp.exp(half - running), 0.0)
        fac_ref[s, 4 * ROWS :, :] = jnp.exp(half)
        before = before + total


def chunk_factors(kv, hl, memories, td):
    g, rows, hd = kv.shape
    return pl.pallas_call(
        functools.partial(factor_kernel, g, hl, memories, td),
        grid=(1,),
        in_specs=chunk_specs(kv, hl, td, 1)[:1],
        out_specs=pl.BlockSpec((g, 5 * ROWS, td), lambda i: (0, 0, 0)),
        out_shape=jax.ShapeDtypeStruct((g, 5 * ROWS, td), F32),
        scratch_shapes=[pltpu.VMEM((g * ROWS, td), F32), pltpu.VMEM((g * ROWS, 2 * td), F32)],
        compiler_params=PARAMS,
        cost_estimate=pl.CostEstimate(flops=g * td * td, bytes_accessed=g * td * 200, transcendentals=0),
        name="chunk_factors",
    )(kv)


def chunk_kernel(hl, memories, td, fac_ref, kv_ref, lhs_ref, st_scr):
    hd = kv_ref.shape[2]

    @pl.when(pl.program_id(0) == 0)
    def _():
        st_scr[...] = jnp.zeros_like(st_scr)

    for n in range(kv_ref.shape[0]):
        for h in range(hl):
            key = kv_ref[n, h * td : (h + 1) * td, :]
            value = kv_ref[n, (hl + h) * td : (hl + h + 1) * td, :].astype(F32)
            for m in range(memories):
                j = h * memories + m
                rows = slice(m * hd, (m + 1) * hd)
                own = fac_ref[n, 4 * ROWS + j : 4 * ROWS + j + 1, :]
                scaled = (value * fac_ref[n, 3 * ROWS + j : 3 * ROWS + j + 1, :]).astype(BF16)
                lhs_ref[n, h, rows, :td] = scaled
                grown = dot(scaled, key)
                state = st_scr[h, rows, :] * own
                lhs_ref[n, h, rows, td:] = state.astype(BF16)
                st_scr[h, rows, :] = (state + grown) * own


def chunk_states(kv, factors, hl, memories, td):
    g, rows, hd = kv.shape
    step = math.gcd(g, 8)
    return pl.pallas_call(
        functools.partial(chunk_kernel, hl, memories, td),
        grid=(g // step,),
        in_specs=[
            pl.BlockSpec((step,) + factors.shape[1:], lambda i: (i, 0, 0)),
            chunk_specs(kv, hl, td, step)[1],
        ],
        out_specs=pl.BlockSpec((step, hl, memories * hd, td + hd), lambda i: (i, 0, 0, 0)),
        out_shape=jax.ShapeDtypeStruct((g, hl, memories * hd, td + hd), BF16),
        scratch_shapes=[pltpu.VMEM((hl, memories * hd, hd), F32)],
        compiler_params=PARAMS,
        cost_estimate=pl.CostEstimate(
            flops=2 * g * td * hl * memories * hd * hd, bytes_accessed=kv.size * 10, transcendentals=0
        ),
        name="chunk_states",
    )(factors, kv)


def readout_kernel(
    hl, memories, lo, td, q_ref, k_ref, lhs_ref, fac_ref, state_ref, gain_ref, out_ref,
    st_scr, gain_scr, acc_scr,
):
    hd = q_ref.shape[3]
    part = q_ref.shape[0]
    i = pl.program_id(0)

    @pl.when(i == 0)
    def _():
        st_scr[...] = state_ref[...].astype(F32)
        place = lax.axis_index("mem") * lo + lax.axis_index("lo")
        for h in range(hl):
            own = gain_ref[pl.ds(place * hl + h, 1), :]
            gain_scr[h] = jnp.broadcast_to(own, (td, hd)).T

    causal = lax.broadcasted_iota(jnp.int32, (td, td), 0) <= lax.broadcasted_iota(jnp.int32, (td, td), 1)
    units = [(a, b, h) for b in range(lo) for a in range(part) for h in range(hl)]
    right = []
    for a, b, h in units:
        query = q_ref[a, b, h * td : (h + 1) * td, :]
        key = k_ref[b, a, h * td : (h + 1) * td, :]
        scores = jnp.where(causal, dot(key, query), 0.0).astype(BF16)
        right.append(jnp.concatenate([scores, query], axis=0))
    for u, (a, b, h) in enumerate(units):
        s = b * memories + i * part + a
        for m in range(memories):
            j = 2 * ROWS + h * memories + m
            rows = slice(m * hd, (m + 1) * hd)
            state = lhs_ref[b, a, h, rows, td:].astype(F32) + st_scr[h, rows, :] * fac_ref[s, j : j + 1, :]
            left = jnp.concatenate([lhs_ref[b, a, h, rows, :td], state.astype(BF16)], axis=1)
            acc_scr[u, rows, :] = dot(left, right[u])
    for u, (a, b, h) in enumerate(units):
        s = b * memories + i * part + a
        mixed = None
        for m in range(memories):
            j = h * memories + m
            read = acc_scr[u, m * hd : (m + 1) * hd, :] * fac_ref[s, j : j + 1, :]
            mean = jnp.sum(read * read, axis=0, keepdims=True) * (1.0 / hd)
            term = read * (lax.rsqrt(mean + 1e-06) * fac_ref[s, ROWS + j : ROWS + j + 1, :])
            mixed = term if mixed is None else mixed + term
        out_ref[a, b, h * td : (h + 1) * td, :] = (mixed * gain_scr[h]).astype(BF16).T


def readout(q, kv, lhs, factors, state, gain, lo, hl, memories, td):
    g, _, hd = q.shape
    part = max(1, math.gcd(memories, 8 // math.gcd(lo, 8)))
    q = q.reshape(memories, lo, hl * td, hd)
    tokens = pl.BlockSpec((part, lo, hl * td, hd), lambda i: (i, 0, 0, 0))
    out = pl.pallas_call(
        functools.partial(readout_kernel, hl, memories, lo, td),
        grid=(memories // part,),
        in_specs=[
            tokens,
            pl.BlockSpec((lo, part, hl * td, hd), lambda i: (0, i, 0, 0)),
            pl.BlockSpec((lo, part) + lhs.shape[1:], lambda i: (0, i, 0, 0, 0)),
            pl.BlockSpec(factors.shape, lambda i: (0, 0, 0)),
            pl.BlockSpec(state.shape, lambda i: (0, 0, 0)),
            pl.BlockSpec(gain.shape, lambda i: (0, 0)),
        ],
        out_specs=tokens,
        out_shape=jax.ShapeDtypeStruct(q.shape, BF16),
        scratch_shapes=[
            pltpu.VMEM(state.shape, F32),
            pltpu.VMEM((hl, hd, td), F32),
            pltpu.VMEM((part * lo * hl, memories * hd, td), F32),
        ],
        compiler_params=PARAMS,
        cost_estimate=pl.CostEstimate(
            flops=8 * g * td * hl * memories * hd * hd, bytes_accessed=kv.size * 10, transcendentals=0
        ),
        name="readout",
    )(
        q,
        kv.reshape((lo, memories) + kv.shape[1:]),
        lhs.reshape((lo, memories) + lhs.shape[1:]),
        factors,
        state,
        gain,
    )
    return out.reshape(g, hl * td, hd)


def entering_state(state, total, groups, hl, memories):
    if groups == 1:
        return jnp.zeros_like(state)
    state = lax.ppermute(state, "hi", [(i, i + 1) for i in range(groups - 1)])
    if groups == 2:
        return state
    factor = lax.ppermute(total[:, :1], "hi", [(i, i + 1) for i in range(groups - 1)])

    def spread(f):
        wide = jnp.broadcast_to(f.reshape(hl, memories, 1), (hl, memories, state.shape[2]))
        return wide.reshape(hl, state.shape[1], 1)

    held = state.astype(F32)
    step = 1
    while step < groups - 1:
        pairs = [(i, i + step) for i in range(groups - step)]
        earlier = lax.ppermute(held.astype(BF16), "hi", pairs).astype(F32)
        earlier_factor = lax.ppermute(factor, "hi", pairs)
        held = held + spread(factor) * earlier
        factor = factor * earlier_factor
        step *= 2
    return held.astype(BF16)


def shards(queries, keys, values, log_decay, routes, route_weight, gain):
    td, heads, hd = queries.shape[1:]
    memories = lax.axis_size("mem")
    lo = lax.axis_size("lo")
    groups = lax.axis_size("hi")
    g = memories * lo
    hl = heads // g
    kv_send, q_send = pack(
        keys[0],
        values[0],
        queries[0],
        log_decay[0].T,
        routes[0].T,
        route_weight[0].T,
        lo,
        memories,
        hl,
    )
    kv_send = kv_send.reshape(g, 2 * hl * td + META, hd)
    kv = lax.all_to_all(kv_send, ("lo", "mem"), split_axis=0, concat_axis=0, tiled=True)
    q = lax.all_to_all(q_send, ("mem", "lo"), split_axis=0, concat_axis=0, tiled=True)
    state, total = local_state(kv, hl, memories, td)
    entering = entering_state(state, total, groups, hl, memories)
    factors = chunk_factors(kv, hl, memories, td)
    lhs = chunk_states(kv, factors, hl, memories, td)
    out = readout(q, kv, lhs, factors, entering, gain.reshape(heads, hd), lo, hl, memories, td)
    back = lax.all_to_all(out, ("mem", "lo"), split_axis=0, concat_axis=0, tiled=True)
    return back.reshape(heads, td, hd).transpose(1, 0, 2)[None]


def solution(mesh):
    memories, blocks = mesh.shape["mem"], mesh.shape["ctx"]
    def call(queries, keys, values, log_decay, routes, route_weight, gain):
        heads = queries.shape[2]
        lo = max(
            s
            for s in range(1, max(1, blocks // 2) + 1)
            if blocks % s == 0 and heads % (memories * s) == 0
        )
        split = Mesh(mesh.devices.reshape(memories, blocks // lo, lo), ("mem", "hi", "lo"))
        tokens = P(("hi", "lo"), "mem")
        return jax.shard_map(
            shards,
            mesh=split,
            in_specs=(tokens,) * 6 + (P(),),
            out_specs=tokens,
            check_vma=False,
        )(queries, keys, values, log_decay, routes, route_weight, gain)

    return call
```

```python
import functools
import math

import jax
import jax.numpy as jnp
from jax import lax
from jax.experimental import pallas as pl
from jax.experimental.pallas import tpu as pltpu
from jax.sharding import Mesh
from jax.sharding import PartitionSpec as P

F32 = jnp.float32
BF16 = jnp.bfloat16
META = 8
RATES = 6
PARAMS = pltpu.CompilerParams(vmem_limit_bytes=50 << 20)
ROWS = 8


def dot(a, b, dims=((1,), (0,))):
    return lax.dot_general(a, b, (dims, ((), ())), preferred_element_type=F32)


def split_heads(src, place, scr, hl, base, turned):
    td, hb, hd = src.shape
    scr[...] = src[...].astype(F32).reshape(td * hb, hd)
    for j in range(hb):
        start = base + (j % hl) * td
        rows = scr[pl.ds(j, td, stride=hb), :].astype(BF16)
        place(j // hl)[start : start + td, :] = rows.T if turned else rows


def pack_kernel(hl, lo, k_ref, v_ref, q_ref, ld_ref, rt_ref, wt_ref, out, q_out, scr_k, scr_v, scr_q, ld_scr):
    i = pl.program_id(0)
    td, hb, _ = k_ref.shape
    place = lambda dd: out.at[dd % lo, dd // lo]

    @pl.when(i == 0)
    def _():
        ld_scr[...] = ld_ref[...].astype(F32)

    split_heads(k_ref, place, scr_k, hl, 0, False)
    split_heads(v_ref, place, scr_v, hl, hl * td, True)
    split_heads(q_ref, lambda dd: q_out.at[dd], scr_q, hl, 0, True)
    w = wt_ref[...]
    hi = w.astype(BF16).astype(F32)
    mid = (w - hi).astype(BF16).astype(F32)
    table = jnp.concatenate([rt_ref[...].astype(F32), hi, mid], axis=0)
    here = ld_scr[pl.ds(pl.multiple_of(i * hb, hb), hb), :]
    for dd in range(hb // hl):
        own = (here if dd == 0 else pltpu.roll(here, hb - dd * hl, 0))[: META - RATES]
        place(dd)[2 * hl * td :, :] = jnp.concatenate([table, own], axis=0).astype(BF16)


def pack(keys, values, queries, ld_t, routes_t, weight_t, lo, memories, hl):
    td, heads, hd = keys.shape
    hb = math.gcd(heads, 16)
    rows = 2 * hl * td + META
    whole = lambda a: pl.BlockSpec(a.shape, lambda i: (0,) * a.ndim)
    block = pl.BlockSpec((td, hb, hd), lambda i: (0, i, 0))
    return pl.pallas_call(
        functools.partial(pack_kernel, hl, lo),
        grid=(heads // hb,),
        in_specs=[block, block, block, whole(ld_t), whole(routes_t), whole(weight_t)],
        out_specs=[
            pl.BlockSpec((lo, hb // hl // lo, rows, hd), lambda i: (0, i, 0, 0)),
            pl.BlockSpec((hb // hl, hl * td, hd), lambda i: (i, 0, 0)),
        ],
        out_shape=[
            jax.ShapeDtypeStruct((lo, memories, rows, hd), BF16),
            jax.ShapeDtypeStruct((lo * memories, hl * td, hd), BF16),
        ],
        scratch_shapes=[pltpu.VMEM((td * hb, hd), F32)] * 3 + [pltpu.VMEM((heads, td), F32)],
        name="pack",
    )(keys, values, queries, ld_t, routes_t, weight_t)


def meta_rows(meta_ref, s, hl, memories):
    meta = meta_ref[s].astype(F32)
    td = meta.shape[1]
    row = lax.broadcasted_iota(jnp.int32, (ROWS, td), 0)
    memory = lax.rem(row, memories).astype(F32)
    first = meta[0:1] == memory
    second = meta[1:2] == memory
    rate = jnp.broadcast_to(meta[RATES : RATES + 1], (ROWS, td))
    for h in range(1, hl):
        rate = jnp.where(row >= h * memories, meta[RATES + h : RATES + h + 1], rate)
    member = first | second
    return meta, first, second, member, jnp.where(member, rate, 0.0)


def running_sums(meta_ref, a_scr, cs_scr, g, hl, memories):
    td = a_scr.shape[1]
    for s in range(g):
        a_scr[s * ROWS : (s + 1) * ROWS, :] = meta_rows(meta_ref, s, hl, memories)[4]
    t0 = lax.broadcasted_iota(jnp.int32, (td, 2 * td), 0)
    t1 = lax.broadcasted_iota(jnp.int32, (td, 2 * td), 1)
    upper = jnp.where(t0 <= t1, 1.0, 0.0).astype(BF16)
    cs_scr[...] = dot(a_scr[...].astype(BF16), upper)


def state_kernel(
    g, hl, memories, td, meta_ref, kv_ref, state_ref, total_ref, a_scr, cs_scr, dec_scr, acc_scr
):
    i = pl.program_id(0)
    step = kv_ref.shape[0]
    hd = kv_ref.shape[2]

    @pl.when(i == 0)
    def _():
        running_sums(meta_ref, a_scr, cs_scr, g, hl, memories)
        after = jnp.zeros((ROWS, td), F32)
        for s in reversed(range(g)):
            member = meta_rows(meta_ref, s, hl, memories)[3]
            rows = slice(s * ROWS, (s + 1) * ROWS)
            running, total = cs_scr[rows, :td], cs_scr[rows, td:]
            dec_scr[s // step, :, s % step * td : (s % step + 1) * td] = jnp.where(
                member, jnp.exp(total - running + after), 0.0
            )
            after = after + total
        total_ref[...] = jnp.exp(after)
        acc_scr[...] = jnp.zeros_like(acc_scr)

    decay = dec_scr[i]
    for h in range(hl):
        key = jnp.concatenate([kv_ref[n, h * td : (h + 1) * td, :] for n in range(step)], axis=0)
        value = jnp.concatenate(
            [kv_ref[n, (hl + h) * td : (hl + h + 1) * td, :] for n in range(step)], axis=1
        ).astype(F32)
        for m in range(memories):
            j = h * memories + m
            acc_scr[h, m * hd : (m + 1) * hd, :] += dot((value * decay[j : j + 1, :]).astype(BF16), key)

    @pl.when(i == pl.num_programs(0) - 1)
    def _():
        state_ref[...] = acc_scr[...].astype(BF16)


def chunk_specs(kv, hl, td, step):
    g, rows, hd = kv.shape
    meta = pl.BlockSpec((g, META, hd), lambda i: (0, 2 * hl * td // META, 0))
    tokens = pl.BlockSpec((step, 2 * hl * td, hd), lambda i: (i, 0, 0))
    return [meta, tokens]


def local_state(kv, hl, memories, td):
    g, rows, hd = kv.shape
    step = math.gcd(g, 16)
    return pl.pallas_call(
        functools.partial(state_kernel, g, hl, memories, td),
        grid=(g // step,),
        in_specs=chunk_specs(kv, hl, td, step),
        out_specs=[
            pl.BlockSpec((hl, memories * hd, hd), lambda i: (0, 0, 0)),
            pl.BlockSpec((ROWS, td), lambda i: (0, 0)),
        ],
        out_shape=[
            jax.ShapeDtypeStruct((hl, memories * hd, hd), BF16),
            jax.ShapeDtypeStruct((ROWS, td), F32),
        ],
        scratch_shapes=[
            pltpu.VMEM((g * ROWS, td), F32),
            pltpu.VMEM((g * ROWS, 2 * td), F32),
            pltpu.VMEM((g // step, ROWS, step * td), F32),
            pltpu.VMEM((hl, memories * hd, hd), F32),
        ],
        compiler_params=PARAMS,
        cost_estimate=pl.CostEstimate(
            flops=2 * g * td * hl * memories * hd * hd, bytes_accessed=kv.size * 2, transcendentals=0
        ),
        name="local_state",
    )(kv, kv)


def factor_kernel(g, hl, memories, td, meta_ref, fac_ref, a_scr, cs_scr):
    scale = meta_ref.shape[2] ** (-0.5)
    running_sums(meta_ref, a_scr, cs_scr, g, hl, memories)
    before = jnp.zeros((ROWS, td), F32)
    for s in range(g):
        meta, first, second, member, _ = meta_rows(meta_ref, s, hl, memories)
        rows = slice(s * ROWS, (s + 1) * ROWS)
        running, total = cs_scr[rows, :td], cs_scr[rows, td:]
        half = 0.5 * total
        weight = [meta[2 + n : 3 + n] + meta[4 + n : 5 + n] for n in range(2)]
        fac_ref[s, 0:ROWS, :] = jnp.exp(running - half) * scale
        fac_ref[s, ROWS : 2 * ROWS, :] = jnp.where(first, weight[0], 0.0) + jnp.where(
            second, weight[1], 0.0
        )
        fac_ref[s, 2 * ROWS : 3 * ROWS, :] = jnp.exp(before + half)
        fac_ref[s, 3 * ROWS : 4 * ROWS, :] = jnp.where(member, jnp.exp(half - running), 0.0)
        fac_ref[s, 4 * ROWS :, :] = jnp.exp(half)
        before = before + total


def chunk_factors(kv, hl, memories, td):
    g, rows, hd = kv.shape
    return pl.pallas_call(
        functools.partial(factor_kernel, g, hl, memories, td),
        grid=(1,),
        in_specs=chunk_specs(kv, hl, td, 1)[:1],
        out_specs=pl.BlockSpec((g, 5 * ROWS, td), lambda i: (0, 0, 0)),
        out_shape=jax.ShapeDtypeStruct((g, 5 * ROWS, td), F32),
        scratch_shapes=[pltpu.VMEM((g * ROWS, td), F32), pltpu.VMEM((g * ROWS, 2 * td), F32)],
        compiler_params=PARAMS,
        cost_estimate=pl.CostEstimate(flops=g * td * td, bytes_accessed=g * td * 200, transcendentals=0),
        name="chunk_factors",
    )(kv)


def chunk_kernel(hl, memories, td, fac_ref, kv_ref, lhs_ref, st_scr):
    hd = kv_ref.shape[2]

    @pl.when(pl.program_id(0) == 0)
    def _():
        st_scr[...] = jnp.zeros_like(st_scr)

    for n in range(kv_ref.shape[0]):
        for h in range(hl):
            key = kv_ref[n, h * td : (h + 1) * td, :]
            value = kv_ref[n, (hl + h) * td : (hl + h + 1) * td, :].astype(F32)
            for m in range(memories):
                j = h * memories + m
                rows = slice(m * hd, (m + 1) * hd)
                own = fac_ref[n, 4 * ROWS + j : 4 * ROWS + j + 1, :]
                scaled = (value * fac_ref[n, 3 * ROWS + j : 3 * ROWS + j + 1, :]).astype(BF16)
                lhs_ref[n, h, rows, :td] = scaled
                grown = dot(scaled, key)
                state = st_scr[h, rows, :] * own
                lhs_ref[n, h, rows, td:] = state.astype(BF16)
                st_scr[h, rows, :] = (state + grown) * own


def chunk_states(kv, factors, hl, memories, td):
    g, rows, hd = kv.shape
    step = math.gcd(g, 8)
    return pl.pallas_call(
        functools.partial(chunk_kernel, hl, memories, td),
        grid=(g // step,),
        in_specs=[
            pl.BlockSpec((step,) + factors.shape[1:], lambda i: (i, 0, 0)),
            chunk_specs(kv, hl, td, step)[1],
        ],
        out_specs=pl.BlockSpec((step, hl, memories * hd, td + hd), lambda i: (i, 0, 0, 0)),
        out_shape=jax.ShapeDtypeStruct((g, hl, memories * hd, td + hd), BF16),
        scratch_shapes=[pltpu.VMEM((hl, memories * hd, hd), F32)],
        compiler_params=PARAMS,
        cost_estimate=pl.CostEstimate(
            flops=2 * g * td * hl * memories * hd * hd, bytes_accessed=kv.size * 10, transcendentals=0
        ),
        name="chunk_states",
    )(factors, kv)


def readout_kernel(
    hl, memories, lo, td, q_ref, k_ref, lhs_ref, fac_ref, state_ref, gain_ref, out_ref,
    st_scr, gain_scr, acc_scr,
):
    hd = q_ref.shape[3]
    part = q_ref.shape[0]
    i = pl.program_id(0)

    @pl.when(i == 0)
    def _():
        st_scr[...] = state_ref[...].astype(F32)
        place = lax.axis_index("mem") * lo + lax.axis_index("lo")
        for h in range(hl):
            own = gain_ref[pl.ds(place * hl + h, 1), :]
            gain_scr[h] = jnp.broadcast_to(own, (td, hd)).T

    causal = lax.broadcasted_iota(jnp.int32, (td, td), 0) <= lax.broadcasted_iota(jnp.int32, (td, td), 1)
    units = [(a, b, h) for b in range(lo) for a in range(part) for h in range(hl)]
    right = []
    for a, b, h in units:
        query = q_ref[a, b, h * td : (h + 1) * td, :]
        key = k_ref[b, a, h * td : (h + 1) * td, :]
        scores = jnp.where(causal, dot(key, query), 0.0).astype(BF16)
        right.append(jnp.concatenate([scores, query], axis=0))
    for u, (a, b, h) in enumerate(units):
        s = b * memories + i * part + a
        for m in range(memories):
            j = 2 * ROWS + h * memories + m
            rows = slice(m * hd, (m + 1) * hd)
            state = lhs_ref[b, a, h, rows, td:].astype(F32) + st_scr[h, rows, :] * fac_ref[s, j : j + 1, :]
            left = jnp.concatenate([lhs_ref[b, a, h, rows, :td], state.astype(BF16)], axis=1)
            acc_scr[u, rows, :] = dot(left, right[u])
    for u, (a, b, h) in enumerate(units):
        s = b * memories + i * part + a
        mixed = None
        for m in range(memories):
            j = h * memories + m
            read = acc_scr[u, m * hd : (m + 1) * hd, :] * fac_ref[s, j : j + 1, :]
            mean = jnp.sum(read * read, axis=0, keepdims=True) * (1.0 / hd)
            term = read * (lax.rsqrt(mean + 1e-06) * fac_ref[s, ROWS + j : ROWS + j + 1, :])
            mixed = term if mixed is None else mixed + term
        out_ref[a, b, h * td : (h + 1) * td, :] = (mixed * gain_scr[h]).astype(BF16).T


def readout(q, kv, lhs, factors, state, gain, lo, hl, memories, td):
    g, _, hd = q.shape
    part = max(1, math.gcd(memories, 8 // math.gcd(lo, 8)))
    q = q.reshape(memories, lo, hl * td, hd)
    tokens = pl.BlockSpec((part, lo, hl * td, hd), lambda i: (i, 0, 0, 0))
    out = pl.pallas_call(
        functools.partial(readout_kernel, hl, memories, lo, td),
        grid=(memories // part,),
        in_specs=[
            tokens,
            pl.BlockSpec((lo, part, hl * td, hd), lambda i: (0, i, 0, 0)),
            pl.BlockSpec((lo, part) + lhs.shape[1:], lambda i: (0, i, 0, 0, 0)),
            pl.BlockSpec(factors.shape, lambda i: (0, 0, 0)),
            pl.BlockSpec(state.shape, lambda i: (0, 0, 0)),
            pl.BlockSpec(gain.shape, lambda i: (0, 0)),
        ],
        out_specs=tokens,
        out_shape=jax.ShapeDtypeStruct(q.shape, BF16),
        scratch_shapes=[
            pltpu.VMEM(state.shape, F32),
            pltpu.VMEM((hl, hd, td), F32),
            pltpu.VMEM((part * lo * hl, memories * hd, td), F32),
        ],
        compiler_params=PARAMS,
        cost_estimate=pl.CostEstimate(
            flops=8 * g * td * hl * memories * hd * hd, bytes_accessed=kv.size * 10, transcendentals=0
        ),
        name="readout",
    )(
        q,
        kv.reshape((lo, memories) + kv.shape[1:]),
        lhs.reshape((lo, memories) + lhs.shape[1:]),
        factors,
        state,
        gain,
    )
    return out.reshape(g, hl * td, hd)


def entering_state(state, total, groups, hl, memories):
    if groups == 1:
        return jnp.zeros_like(state)
    state = lax.ppermute(state, "hi", [(i, i + 1) for i in range(groups - 1)])
    if groups == 2:
        return state
    factor = lax.ppermute(total[:, :1], "hi", [(i, i + 1) for i in range(groups - 1)])

    def spread(f):
        wide = jnp.broadcast_to(f.reshape(hl, memories, 1), (hl, memories, state.shape[2]))
        return wide.reshape(hl, state.shape[1], 1)

    held = state.astype(F32)
    step = 1
    while step < groups - 1:
        pairs = [(i, i + step) for i in range(groups - step)]
        earlier = lax.ppermute(held.astype(BF16), "hi", pairs).astype(F32)
        earlier_factor = lax.ppermute(factor, "hi", pairs)
        held = held + spread(factor) * earlier
        factor = factor * earlier_factor
        step *= 2
    return held.astype(BF16)


def shards(queries, keys, values, log_decay, routes, route_weight, gain):
    td, heads, hd = queries.shape[1:]
    memories = lax.axis_size("mem")
    lo = lax.axis_size("lo")
    groups = lax.axis_size("hi")
    g = memories * lo
    hl = heads // g
    assert hl <= META - RATES and hl * memories == ROWS
    kv_send, q_send = pack(
        keys[0],
        values[0],
        queries[0],
        log_decay[0].T,
        routes[0].T,
        route_weight[0].T,
        lo,
        memories,
        hl,
    )
    kv_send = kv_send.reshape(g, 2 * hl * td + META, hd)
    kv = lax.all_to_all(kv_send, ("lo", "mem"), split_axis=0, concat_axis=0, tiled=True)
    q = lax.all_to_all(q_send, ("mem", "lo"), split_axis=0, concat_axis=0, tiled=True)
    state, total = local_state(kv, hl, memories, td)
    entering = entering_state(state, total, groups, hl, memories)
    factors = chunk_factors(kv, hl, memories, td)
    lhs = chunk_states(kv, factors, hl, memories, td)
    out = readout(q, kv, lhs, factors, entering, gain.reshape(heads, hd), lo, hl, memories, td)
    back = lax.all_to_all(out, ("mem", "lo"), split_axis=0, concat_axis=0, tiled=True)
    return back.reshape(heads, td, hd).transpose(1, 0, 2)[None]


def solution(mesh):
    memories, blocks = mesh.shape["mem"], mesh.shape["ctx"]
    def call(queries, keys, values, log_decay, routes, route_weight, gain):
        heads = queries.shape[2]
        lo = max(
            s
            for s in range(1, max(1, blocks // 2) + 1)
            if blocks % s == 0 and heads % (memories * s) == 0
        )
        split = Mesh(mesh.devices.reshape(memories, blocks // lo, lo), ("mem", "hi", "lo"))
        tokens = P(("hi", "lo"), "mem")
        return jax.shard_map(
            shards,
            mesh=split,
            in_specs=(tokens,) * 6 + (P(),),
            out_specs=tokens,
            check_vma=False,
        )(queries, keys, values, log_decay, routes, route_weight, gain)

    return call
```

```python
import functools
import math

import jax
import jax.numpy as jnp
from jax import lax
from jax.experimental import pallas as pl
from jax.experimental.pallas import tpu as pltpu
from jax.sharding import Mesh
from jax.sharding import PartitionSpec as P

F32 = jnp.float32
BF16 = jnp.bfloat16
META = 8
RATES = 6
PARAMS = pltpu.CompilerParams(vmem_limit_bytes=50 << 20)
ROWS = 8


def dot(a, b, dims=((1,), (0,))):
    return lax.dot_general(a, b, (dims, ((), ())), preferred_element_type=F32)


def split_heads(src, place, scr, hl, base, turned):
    td, hb, hd = src.shape
    scr[...] = src[...].astype(F32).reshape(td * hb, hd)
    for j in range(hb):
        start = base + (j % hl) * td
        rows = scr[pl.ds(j, td, stride=hb), :].astype(BF16)
        place(j // hl)[start : start + td, :] = rows.T if turned else rows


def pack_kernel(hl, lo, k_ref, v_ref, q_ref, ld_ref, rt_ref, wt_ref, out, q_out, scr_k, scr_v, scr_q, ld_scr):
    i = pl.program_id(0)
    td, hb, _ = k_ref.shape
    place = lambda dd: out.at[dd % lo, dd // lo]

    @pl.when(i == 0)
    def _():
        ld_scr[...] = ld_ref[...].astype(F32)

    split_heads(k_ref, place, scr_k, hl, 0, False)
    split_heads(v_ref, place, scr_v, hl, hl * td, True)
    split_heads(q_ref, lambda dd: q_out.at[dd], scr_q, hl, 0, True)
    w = wt_ref[...]
    hi = w.astype(BF16).astype(F32)
    mid = (w - hi).astype(BF16).astype(F32)
    table = jnp.concatenate([rt_ref[...].astype(F32), hi, mid], axis=0)
    here = ld_scr[pl.ds(pl.multiple_of(i * hb, hb), hb), :]
    for dd in range(hb // hl):
        own = (here if dd == 0 else pltpu.roll(here, hb - dd * hl, 0))[: META - RATES]
        place(dd)[2 * hl * td :, :] = jnp.concatenate([table, own], axis=0).astype(BF16)


def pack(keys, values, queries, ld_t, routes_t, weight_t, lo, memories, hl):
    td, heads, hd = keys.shape
    hb = math.gcd(heads, 16)
    rows = 2 * hl * td + META
    whole = lambda a: pl.BlockSpec(a.shape, lambda i: (0,) * a.ndim)
    block = pl.BlockSpec((td, hb, hd), lambda i: (0, i, 0))
    return pl.pallas_call(
        functools.partial(pack_kernel, hl, lo),
        grid=(heads // hb,),
        in_specs=[block, block, block, whole(ld_t), whole(routes_t), whole(weight_t)],
        out_specs=[
            pl.BlockSpec((lo, hb // hl // lo, rows, hd), lambda i: (0, i, 0, 0)),
            pl.BlockSpec((hb // hl, hl * td, hd), lambda i: (i, 0, 0)),
        ],
        out_shape=[
            jax.ShapeDtypeStruct((lo, memories, rows, hd), BF16),
            jax.ShapeDtypeStruct((lo * memories, hl * td, hd), BF16),
        ],
        scratch_shapes=[pltpu.VMEM((td * hb, hd), F32)] * 3 + [pltpu.VMEM((heads, td), F32)],
        name="pack",
    )(keys, values, queries, ld_t, routes_t, weight_t)


def meta_rows(meta_ref, s, hl, memories):
    meta = meta_ref[s].astype(F32)
    td = meta.shape[1]
    row = lax.broadcasted_iota(jnp.int32, (ROWS, td), 0)
    memory = lax.rem(row, memories).astype(F32)
    first = meta[0:1] == memory
    second = meta[1:2] == memory
    rate = jnp.broadcast_to(meta[RATES : RATES + 1], (ROWS, td))
    for h in range(1, hl):
        rate = jnp.where(row >= h * memories, meta[RATES + h : RATES + h + 1], rate)
    member = first | second
    return meta, first, second, member, jnp.where(member, rate, 0.0)


def running_sums(meta_ref, a_scr, cs_scr, g, hl, memories):
    td = a_scr.shape[1]
    for s in range(g):
        a_scr[s * ROWS : (s + 1) * ROWS, :] = meta_rows(meta_ref, s, hl, memories)[4]
    t0 = lax.broadcasted_iota(jnp.int32, (td, 2 * td), 0)
    t1 = lax.broadcasted_iota(jnp.int32, (td, 2 * td), 1)
    upper = jnp.where(t0 <= t1, 1.0, 0.0).astype(BF16)
    cs_scr[...] = dot(a_scr[...].astype(BF16), upper)


def state_kernel(
    g, hl, memories, td, meta_ref, kv_ref, state_ref, total_ref, a_scr, cs_scr, dec_scr, acc_scr
):
    i = pl.program_id(0)
    step = kv_ref.shape[0]
    hd = kv_ref.shape[2]

    @pl.when(i == 0)
    def _():
        running_sums(meta_ref, a_scr, cs_scr, g, hl, memories)
        after = jnp.zeros((ROWS, td), F32)
        for s in reversed(range(g)):
            member = meta_rows(meta_ref, s, hl, memories)[3]
            rows = slice(s * ROWS, (s + 1) * ROWS)
            running, total = cs_scr[rows, :td], cs_scr[rows, td:]
            dec_scr[s // step, :, s % step * td : (s % step + 1) * td] = jnp.where(
                member, jnp.exp(total - running + after), 0.0
            )
            after = after + total
        total_ref[...] = jnp.exp(after)
        if step < g:
            acc_scr[...] = jnp.zeros_like(acc_scr)

    decay = dec_scr[i]
    for h in range(hl):
        key = jnp.concatenate([kv_ref[n, h * td : (h + 1) * td, :] for n in range(step)], axis=0)
        value = jnp.concatenate(
            [kv_ref[n, (hl + h) * td : (hl + h + 1) * td, :] for n in range(step)], axis=1
        ).astype(F32)
        for m in range(memories):
            j = h * memories + m
            rows = slice(m * hd, (m + 1) * hd)
            grown = dot((value * decay[j : j + 1, :]).astype(BF16), key)
            if step == g:
                state_ref[h, rows, :] = grown.astype(BF16)
            else:
                acc_scr[h, rows, :] += grown

    if step < g:

        @pl.when(i == pl.num_programs(0) - 1)
        def _():
            state_ref[...] = acc_scr[...].astype(BF16)


def chunk_specs(kv, hl, td, step):
    g, rows, hd = kv.shape
    meta = pl.BlockSpec((g, META, hd), lambda i: (0, 2 * hl * td // META, 0))
    tokens = pl.BlockSpec((step, 2 * hl * td, hd), lambda i: (i, 0, 0))
    return [meta, tokens]


def local_state(kv, hl, memories, td):
    g, rows, hd = kv.shape
    step = math.gcd(g, 16)
    return pl.pallas_call(
        functools.partial(state_kernel, g, hl, memories, td),
        grid=(g // step,),
        in_specs=chunk_specs(kv, hl, td, step),
        out_specs=[
            pl.BlockSpec((hl, memories * hd, hd), lambda i: (0, 0, 0)),
            pl.BlockSpec((ROWS, td), lambda i: (0, 0)),
        ],
        out_shape=[
            jax.ShapeDtypeStruct((hl, memories * hd, hd), BF16),
            jax.ShapeDtypeStruct((ROWS, td), F32),
        ],
        scratch_shapes=[
            pltpu.VMEM((g * ROWS, td), F32),
            pltpu.VMEM((g * ROWS, 2 * td), F32),
            pltpu.VMEM((g // step, ROWS, step * td), F32),
            pltpu.VMEM((hl, memories * hd, hd), F32),
        ],
        compiler_params=PARAMS,
        cost_estimate=pl.CostEstimate(
            flops=2 * g * td * hl * memories * hd * hd, bytes_accessed=kv.size * 2, transcendentals=0
        ),
        name="local_state",
    )(kv, kv)


def factor_kernel(g, hl, memories, td, meta_ref, fac_ref, a_scr, cs_scr):
    scale = meta_ref.shape[2] ** (-0.5)
    running_sums(meta_ref, a_scr, cs_scr, g, hl, memories)
    before = jnp.zeros((ROWS, td), F32)
    for s in range(g):
        meta, first, second, member, _ = meta_rows(meta_ref, s, hl, memories)
        rows = slice(s * ROWS, (s + 1) * ROWS)
        running, total = cs_scr[rows, :td], cs_scr[rows, td:]
        half = 0.5 * total
        weight = [meta[2 + n : 3 + n] + meta[4 + n : 5 + n] for n in range(2)]
        fac_ref[s, 0:ROWS, :] = jnp.exp(running - half) * scale
        fac_ref[s, ROWS : 2 * ROWS, :] = jnp.where(first, weight[0], 0.0) + jnp.where(
            second, weight[1], 0.0
        )
        fac_ref[s, 2 * ROWS : 3 * ROWS, :] = jnp.exp(before + half)
        fac_ref[s, 3 * ROWS : 4 * ROWS, :] = jnp.where(member, jnp.exp(half - running), 0.0)
        fac_ref[s, 4 * ROWS :, :] = jnp.exp(half)
        before = before + total


def chunk_factors(kv, hl, memories, td):
    g, rows, hd = kv.shape
    return pl.pallas_call(
        functools.partial(factor_kernel, g, hl, memories, td),
        grid=(1,),
        in_specs=chunk_specs(kv, hl, td, 1)[:1],
        out_specs=pl.BlockSpec((g, 5 * ROWS, td), lambda i: (0, 0, 0)),
        out_shape=jax.ShapeDtypeStruct((g, 5 * ROWS, td), F32),
        scratch_shapes=[pltpu.VMEM((g * ROWS, td), F32), pltpu.VMEM((g * ROWS, 2 * td), F32)],
        compiler_params=PARAMS,
        cost_estimate=pl.CostEstimate(flops=g * td * td, bytes_accessed=g * td * 200, transcendentals=0),
        name="chunk_factors",
    )(kv)


def chunk_kernel(hl, memories, td, fac_ref, kv_ref, lhs_ref, st_scr):
    hd = kv_ref.shape[2]

    @pl.when(pl.program_id(0) == 0)
    def _():
        st_scr[...] = jnp.zeros_like(st_scr)

    for n in range(kv_ref.shape[0]):
        for h in range(hl):
            key = kv_ref[n, h * td : (h + 1) * td, :]
            value = kv_ref[n, (hl + h) * td : (hl + h + 1) * td, :].astype(F32)
            for m in range(memories):
                j = h * memories + m
                rows = slice(m * hd, (m + 1) * hd)
                own = fac_ref[n, 4 * ROWS + j : 4 * ROWS + j + 1, :]
                scaled = (value * fac_ref[n, 3 * ROWS + j : 3 * ROWS + j + 1, :]).astype(BF16)
                lhs_ref[n, h, rows, :td] = scaled
                grown = dot(scaled, key)
                state = st_scr[h, rows, :] * own
                lhs_ref[n, h, rows, td:] = state.astype(BF16)
                st_scr[h, rows, :] = (state + grown) * own


def chunk_states(kv, factors, hl, memories, td):
    g, rows, hd = kv.shape
    step = math.gcd(g, 8)
    return pl.pallas_call(
        functools.partial(chunk_kernel, hl, memories, td),
        grid=(g // step,),
        in_specs=[
            pl.BlockSpec((step,) + factors.shape[1:], lambda i: (i, 0, 0)),
            chunk_specs(kv, hl, td, step)[1],
        ],
        out_specs=pl.BlockSpec((step, hl, memories * hd, td + hd), lambda i: (i, 0, 0, 0)),
        out_shape=jax.ShapeDtypeStruct((g, hl, memories * hd, td + hd), BF16),
        scratch_shapes=[pltpu.VMEM((hl, memories * hd, hd), F32)],
        compiler_params=PARAMS,
        cost_estimate=pl.CostEstimate(
            flops=2 * g * td * hl * memories * hd * hd, bytes_accessed=kv.size * 10, transcendentals=0
        ),
        name="chunk_states",
    )(factors, kv)


def readout_kernel(
    hl, memories, lo, td, q_ref, k_ref, lhs_ref, fac_ref, state_ref, gain_ref, out_ref,
    st_scr, gain_scr, acc_scr,
):
    hd = q_ref.shape[3]
    part = q_ref.shape[0]
    i = pl.program_id(0)

    @pl.when(i == 0)
    def _():
        st_scr[...] = state_ref[...].astype(F32)
        place = lax.axis_index("mem") * lo + lax.axis_index("lo")
        for h in range(hl):
            own = gain_ref[pl.ds(place * hl + h, 1), :]
            gain_scr[h] = jnp.broadcast_to(own, (td, hd)).T

    causal = lax.broadcasted_iota(jnp.int32, (td, td), 0) <= lax.broadcasted_iota(jnp.int32, (td, td), 1)
    units = [(a, b, h) for b in range(lo) for a in range(part) for h in range(hl)]
    right = []
    for a, b, h in units:
        query = q_ref[a, b, h * td : (h + 1) * td, :]
        key = k_ref[b, a, h * td : (h + 1) * td, :]
        scores = jnp.where(causal, dot(key, query), 0.0).astype(BF16)
        right.append(jnp.concatenate([scores, query], axis=0))
    for u, (a, b, h) in enumerate(units):
        s = b * memories + i * part + a
        for m in range(memories):
            j = 2 * ROWS + h * memories + m
            rows = slice(m * hd, (m + 1) * hd)
            state = lhs_ref[b, a, h, rows, td:].astype(F32) + st_scr[h, rows, :] * fac_ref[s, j : j + 1, :]
            left = jnp.concatenate([lhs_ref[b, a, h, rows, :td], state.astype(BF16)], axis=1)
            acc_scr[u, rows, :] = dot(left, right[u])
    for u, (a, b, h) in enumerate(units):
        s = b * memories + i * part + a
        mixed = None
        for m in range(memories):
            j = h * memories + m
            read = acc_scr[u, m * hd : (m + 1) * hd, :] * fac_ref[s, j : j + 1, :]
            mean = jnp.sum(read * read, axis=0, keepdims=True) * (1.0 / hd)
            term = read * (lax.rsqrt(mean + 1e-06) * fac_ref[s, ROWS + j : ROWS + j + 1, :])
            mixed = term if mixed is None else mixed + term
        out_ref[a, b, h * td : (h + 1) * td, :] = (mixed * gain_scr[h]).astype(BF16).T


def readout(q, kv, lhs, factors, state, gain, lo, hl, memories, td):
    g, _, hd = q.shape
    part = max(1, math.gcd(memories, 8 // math.gcd(lo, 8)))
    q = q.reshape(memories, lo, hl * td, hd)
    tokens = pl.BlockSpec((part, lo, hl * td, hd), lambda i: (i, 0, 0, 0))
    out = pl.pallas_call(
        functools.partial(readout_kernel, hl, memories, lo, td),
        grid=(memories // part,),
        in_specs=[
            tokens,
            pl.BlockSpec((lo, part, hl * td, hd), lambda i: (0, i, 0, 0)),
            pl.BlockSpec((lo, part) + lhs.shape[1:], lambda i: (0, i, 0, 0, 0)),
            pl.BlockSpec(factors.shape, lambda i: (0, 0, 0)),
            pl.BlockSpec(state.shape, lambda i: (0, 0, 0)),
            pl.BlockSpec(gain.shape, lambda i: (0, 0)),
        ],
        out_specs=tokens,
        out_shape=jax.ShapeDtypeStruct(q.shape, BF16),
        scratch_shapes=[
            pltpu.VMEM(state.shape, F32),
            pltpu.VMEM((hl, hd, td), F32),
            pltpu.VMEM((part * lo * hl, memories * hd, td), F32),
        ],
        compiler_params=PARAMS,
        cost_estimate=pl.CostEstimate(
            flops=8 * g * td * hl * memories * hd * hd, bytes_accessed=kv.size * 10, transcendentals=0
        ),
        name="readout",
    )(
        q,
        kv.reshape((lo, memories) + kv.shape[1:]),
        lhs.reshape((lo, memories) + lhs.shape[1:]),
        factors,
        state,
        gain,
    )
    return out.reshape(g, hl * td, hd)


def entering_state(state, total, groups, hl, memories):
    if groups == 1:
        return jnp.zeros_like(state)
    state = lax.ppermute(state, "hi", [(i, i + 1) for i in range(groups - 1)])
    if groups == 2:
        return state
    factor = lax.ppermute(total[:, :1], "hi", [(i, i + 1) for i in range(groups - 1)])

    def spread(f):
        wide = jnp.broadcast_to(f.reshape(hl, memories, 1), (hl, memories, state.shape[2]))
        return wide.reshape(hl, state.shape[1], 1)

    held = state.astype(F32)
    step = 1
    while step < groups - 1:
        pairs = [(i, i + step) for i in range(groups - step)]
        earlier = lax.ppermute(held.astype(BF16), "hi", pairs).astype(F32)
        earlier_factor = lax.ppermute(factor, "hi", pairs)
        held = held + spread(factor) * earlier
        factor = factor * earlier_factor
        step *= 2
    return held.astype(BF16)


def shards(queries, keys, values, log_decay, routes, route_weight, gain):
    td, heads, hd = queries.shape[1:]
    memories = lax.axis_size("mem")
    lo = lax.axis_size("lo")
    groups = lax.axis_size("hi")
    g = memories * lo
    hl = heads // g
    assert hl <= META - RATES and hl * memories == ROWS
    kv_send, q_send = pack(
        keys[0],
        values[0],
        queries[0],
        log_decay[0].T,
        routes[0].T,
        route_weight[0].T,
        lo,
        memories,
        hl,
    )
    kv_send = kv_send.reshape(g, 2 * hl * td + META, hd)
    kv = lax.all_to_all(kv_send, ("lo", "mem"), split_axis=0, concat_axis=0, tiled=True)
    q = lax.all_to_all(q_send, ("mem", "lo"), split_axis=0, concat_axis=0, tiled=True)
    state, total = local_state(kv, hl, memories, td)
    entering = entering_state(state, total, groups, hl, memories)
    factors = chunk_factors(kv, hl, memories, td)
    lhs = chunk_states(kv, factors, hl, memories, td)
    out = readout(q, kv, lhs, factors, entering, gain.reshape(heads, hd), lo, hl, memories, td)
    back = lax.all_to_all(out, ("mem", "lo"), split_axis=0, concat_axis=0, tiled=True)
    return back.reshape(heads, td, hd).transpose(1, 0, 2)[None]


def solution(mesh):
    memories, blocks = mesh.shape["mem"], mesh.shape["ctx"]
    def call(queries, keys, values, log_decay, routes, route_weight, gain):
        heads = queries.shape[2]
        lo = max(
            s
            for s in range(1, max(1, blocks // 2) + 1)
            if blocks % s == 0 and heads % (memories * s) == 0
        )
        split = Mesh(mesh.devices.reshape(memories, blocks // lo, lo), ("mem", "hi", "lo"))
        tokens = P(("hi", "lo"), "mem")
        return jax.shard_map(
            shards,
            mesh=split,
            in_specs=(tokens,) * 6 + (P(),),
            out_specs=tokens,
            check_vma=False,
        )(queries, keys, values, log_decay, routes, route_weight, gain)

    return call
```

```python
import functools
import math

import jax
import jax.numpy as jnp
from jax import lax
from jax.experimental import pallas as pl
from jax.experimental.pallas import tpu as pltpu
from jax.sharding import Mesh
from jax.sharding import PartitionSpec as P

F32 = jnp.float32
BF16 = jnp.bfloat16
META = 8
RATES = 6
PARAMS = pltpu.CompilerParams(vmem_limit_bytes=50 << 20)
ROWS = 8


def dot(a, b, dims=((1,), (0,))):
    return lax.dot_general(a, b, (dims, ((), ())), preferred_element_type=F32)


def split_heads(src, place, scr, hl, base, turned):
    td, hb, hd = src.shape
    scr[...] = src[...].astype(F32).reshape(td * hb, hd)
    for j in range(hb):
        start = base + (j % hl) * td
        rows = scr[pl.ds(j, td, stride=hb), :].astype(BF16)
        place(j // hl)[start : start + td, :] = rows.T if turned else rows


def pack_kernel(hl, lo, k_ref, v_ref, q_ref, ld_ref, rt_ref, wt_ref, out, q_out, scr_k, scr_v, scr_q, ld_scr):
    i = pl.program_id(0)
    td, hb, _ = k_ref.shape
    place = lambda dd: out.at[dd % lo, dd // lo]

    @pl.when(i == 0)
    def _():
        ld_scr[...] = ld_ref[...].astype(F32)

    split_heads(k_ref, place, scr_k, hl, 0, False)
    split_heads(v_ref, place, scr_v, hl, hl * td, True)
    split_heads(q_ref, lambda dd: q_out.at[dd], scr_q, hl, 0, True)
    w = wt_ref[...]
    hi = w.astype(BF16).astype(F32)
    mid = (w - hi).astype(BF16).astype(F32)
    table = jnp.concatenate([rt_ref[...].astype(F32), hi, mid], axis=0)
    here = ld_scr[pl.ds(pl.multiple_of(i * hb, hb), hb), :]
    for dd in range(hb // hl):
        own = (here if dd == 0 else pltpu.roll(here, hb - dd * hl, 0))[: META - RATES]
        place(dd)[2 * hl * td :, :] = jnp.concatenate([table, own], axis=0).astype(BF16)


def pack(keys, values, queries, ld_t, routes_t, weight_t, lo, memories, hl):
    td, heads, hd = keys.shape
    hb = math.gcd(heads, 16)
    rows = 2 * hl * td + META
    whole = lambda a: pl.BlockSpec(a.shape, lambda i: (0,) * a.ndim)
    block = pl.BlockSpec((td, hb, hd), lambda i: (0, i, 0))
    return pl.pallas_call(
        functools.partial(pack_kernel, hl, lo),
        grid=(heads // hb,),
        in_specs=[block, block, block, whole(ld_t), whole(routes_t), whole(weight_t)],
        out_specs=[
            pl.BlockSpec((lo, hb // hl // lo, rows, hd), lambda i: (0, i, 0, 0)),
            pl.BlockSpec((hb // hl, hl * td, hd), lambda i: (i, 0, 0)),
        ],
        out_shape=[
            jax.ShapeDtypeStruct((lo, memories, rows, hd), BF16),
            jax.ShapeDtypeStruct((lo * memories, hl * td, hd), BF16),
        ],
        scratch_shapes=[pltpu.VMEM((td * hb, hd), F32)] * 3 + [pltpu.VMEM((heads, td), F32)],
        name="pack",
    )(keys, values, queries, ld_t, routes_t, weight_t)


def meta_rows(meta_ref, s, hl, memories):
    meta = meta_ref[s].astype(F32)
    td = meta.shape[1]
    row = lax.broadcasted_iota(jnp.int32, (ROWS, td), 0)
    memory = lax.rem(row, memories).astype(F32)
    first = meta[0:1] == memory
    second = meta[1:2] == memory
    rate = jnp.broadcast_to(meta[RATES : RATES + 1], (ROWS, td))
    for h in range(1, hl):
        rate = jnp.where(row >= h * memories, meta[RATES + h : RATES + h + 1], rate)
    member = first | second
    return meta, first, second, member, jnp.where(member, rate, 0.0)


def running_sums(meta_ref, a_scr, cs_scr, g, hl, memories):
    td = a_scr.shape[1]
    for s in range(g):
        a_scr[s * ROWS : (s + 1) * ROWS, :] = meta_rows(meta_ref, s, hl, memories)[4]
    t0 = lax.broadcasted_iota(jnp.int32, (td, 2 * td), 0)
    t1 = lax.broadcasted_iota(jnp.int32, (td, 2 * td), 1)
    upper = jnp.where(t0 <= t1, 1.0, 0.0).astype(BF16)
    cs_scr[...] = dot(a_scr[...].astype(BF16), upper)


def state_kernel(
    g, hl, memories, td, meta_ref, kv_ref, state_ref, total_ref, a_scr, cs_scr, dec_scr, acc_scr
):
    i = pl.program_id(0)
    step = kv_ref.shape[0]
    hd = kv_ref.shape[2]

    @pl.when(i == 0)
    def _():
        running_sums(meta_ref, a_scr, cs_scr, g, hl, memories)
        after = jnp.zeros((ROWS, td), F32)
        for s in reversed(range(g)):
            member = meta_rows(meta_ref, s, hl, memories)[3]
            rows = slice(s * ROWS, (s + 1) * ROWS)
            running, total = cs_scr[rows, :td], cs_scr[rows, td:]
            dec_scr[s // step, :, s % step * td : (s % step + 1) * td] = jnp.where(
                member, jnp.exp(total - running + after), 0.0
            )
            after = after + total
        total_ref[...] = jnp.exp(after)
        if step < g:
            acc_scr[...] = jnp.zeros_like(acc_scr)

    decay = dec_scr[i]
    for h in range(hl):
        key = jnp.concatenate([kv_ref[n, h * td : (h + 1) * td, :] for n in range(step)], axis=0)
        value = jnp.concatenate(
            [kv_ref[n, (hl + h) * td : (hl + h + 1) * td, :] for n in range(step)], axis=1
        ).astype(F32)
        for m in range(memories):
            j = h * memories + m
            rows = slice(m * hd, (m + 1) * hd)
            grown = dot((value * decay[j : j + 1, :]).astype(BF16), key)
            if step == g:
                state_ref[h, rows, :] = grown.astype(BF16)
            else:
                acc_scr[h, rows, :] += grown

    if step < g:

        @pl.when(i == pl.num_programs(0) - 1)
        def _():
            state_ref[...] = acc_scr[...].astype(BF16)


def chunk_specs(kv, hl, td, step):
    g, rows, hd = kv.shape
    meta = pl.BlockSpec((g, META, hd), lambda i: (0, 2 * hl * td // META, 0))
    tokens = pl.BlockSpec((step, 2 * hl * td, hd), lambda i: (i, 0, 0))
    return [meta, tokens]


def local_state(kv, hl, memories, td):
    g, rows, hd = kv.shape
    step = math.gcd(g, 16)
    return pl.pallas_call(
        functools.partial(state_kernel, g, hl, memories, td),
        grid=(g // step,),
        in_specs=chunk_specs(kv, hl, td, step),
        out_specs=[
            pl.BlockSpec((hl, memories * hd, hd), lambda i: (0, 0, 0)),
            pl.BlockSpec((ROWS, td), lambda i: (0, 0)),
        ],
        out_shape=[
            jax.ShapeDtypeStruct((hl, memories * hd, hd), BF16),
            jax.ShapeDtypeStruct((ROWS, td), F32),
        ],
        scratch_shapes=[
            pltpu.VMEM((g * ROWS, td), F32),
            pltpu.VMEM((g * ROWS, 2 * td), F32),
            pltpu.VMEM((g // step, ROWS, step * td), F32),
            pltpu.VMEM((hl, memories * hd, hd), F32),
        ],
        compiler_params=PARAMS,
        cost_estimate=pl.CostEstimate(
            flops=2 * g * td * hl * memories * hd * hd, bytes_accessed=kv.size * 2, transcendentals=0
        ),
        name="local_state",
    )(kv, kv)


def factor_kernel(g, hl, memories, td, meta_ref, fac_ref, a_scr, cs_scr):
    scale = meta_ref.shape[2] ** (-0.5)
    running_sums(meta_ref, a_scr, cs_scr, g, hl, memories)
    before = jnp.zeros((ROWS, td), F32)
    for s in range(g):
        meta, first, second, member, _ = meta_rows(meta_ref, s, hl, memories)
        rows = slice(s * ROWS, (s + 1) * ROWS)
        running, total = cs_scr[rows, :td], cs_scr[rows, td:]
        half = 0.5 * total
        weight = [meta[2 + n : 3 + n] + meta[4 + n : 5 + n] for n in range(2)]
        fac_ref[s, 0:ROWS, :] = jnp.exp(running - half) * scale
        fac_ref[s, ROWS : 2 * ROWS, :] = jnp.where(first, weight[0], 0.0) + jnp.where(
            second, weight[1], 0.0
        )
        fac_ref[s, 2 * ROWS : 3 * ROWS, :] = jnp.exp(before + half)
        fac_ref[s, 3 * ROWS : 4 * ROWS, :] = jnp.where(member, jnp.exp(half - running), 0.0)
        fac_ref[s, 4 * ROWS :, :] = jnp.exp(half)
        before = before + total


def chunk_factors(kv, hl, memories, td):
    g, rows, hd = kv.shape
    return pl.pallas_call(
        functools.partial(factor_kernel, g, hl, memories, td),
        grid=(1,),
        in_specs=chunk_specs(kv, hl, td, 1)[:1],
        out_specs=pl.BlockSpec((g, 5 * ROWS, td), lambda i: (0, 0, 0)),
        out_shape=jax.ShapeDtypeStruct((g, 5 * ROWS, td), F32),
        scratch_shapes=[pltpu.VMEM((g * ROWS, td), F32), pltpu.VMEM((g * ROWS, 2 * td), F32)],
        compiler_params=PARAMS,
        cost_estimate=pl.CostEstimate(flops=g * td * td, bytes_accessed=g * td * 200, transcendentals=0),
        name="chunk_factors",
    )(kv)


def chunk_kernel(hl, memories, td, fac_ref, kv_ref, lhs_ref, st_scr):
    hd = kv_ref.shape[2]

    @pl.when(pl.program_id(0) == 0)
    def _():
        st_scr[...] = jnp.zeros_like(st_scr)

    for n in range(kv_ref.shape[0]):
        for h in range(hl):
            key = kv_ref[n, h * td : (h + 1) * td, :]
            value = kv_ref[n, (hl + h) * td : (hl + h + 1) * td, :].astype(F32)
            for m in range(memories):
                j = h * memories + m
                rows = slice(m * hd, (m + 1) * hd)
                own = fac_ref[n, 4 * ROWS + j : 4 * ROWS + j + 1, :]
                scaled = (value * fac_ref[n, 3 * ROWS + j : 3 * ROWS + j + 1, :]).astype(BF16)
                lhs_ref[n, h, rows, :td] = scaled
                grown = dot(scaled, key)
                state = st_scr[h, rows, :] * own
                lhs_ref[n, h, rows, td:] = state.astype(BF16)
                st_scr[h, rows, :] = (state + grown) * own


def chunk_states(kv, factors, hl, memories, td):
    g, rows, hd = kv.shape
    step = math.gcd(g, 8)
    return pl.pallas_call(
        functools.partial(chunk_kernel, hl, memories, td),
        grid=(g // step,),
        in_specs=[
            pl.BlockSpec((step,) + factors.shape[1:], lambda i: (i, 0, 0)),
            chunk_specs(kv, hl, td, step)[1],
        ],
        out_specs=pl.BlockSpec((step, hl, memories * hd, td + hd), lambda i: (i, 0, 0, 0)),
        out_shape=jax.ShapeDtypeStruct((g, hl, memories * hd, td + hd), BF16),
        scratch_shapes=[pltpu.VMEM((hl, memories * hd, hd), F32)],
        compiler_params=PARAMS,
        cost_estimate=pl.CostEstimate(
            flops=2 * g * td * hl * memories * hd * hd, bytes_accessed=kv.size * 10, transcendentals=0
        ),
        name="chunk_states",
    )(factors, kv)


def readout_kernel(
    hl, memories, lo, td, q_ref, k_ref, lhs_ref, fac_ref, state_ref, gain_ref, out_ref,
    st_scr, gain_scr, acc_scr,
):
    hd = q_ref.shape[3]
    part = q_ref.shape[0]
    i = pl.program_id(0)

    @pl.when(i == 0)
    def _():
        st_scr[...] = state_ref[...].astype(F32)
        place = lax.axis_index("mem") * lo + lax.axis_index("lo")
        for h in range(hl):
            own = gain_ref[pl.ds(place * hl + h, 1), :]
            gain_scr[h] = jnp.broadcast_to(own, (td, hd)).T

    causal = lax.broadcasted_iota(jnp.int32, (td, td), 0) <= lax.broadcasted_iota(jnp.int32, (td, td), 1)
    units = [(a, b, h) for b in range(lo) for a in range(part) for h in range(hl)]
    right = {}

    def score(u):
        a, b, h = units[u]
        query = q_ref[a, b, h * td : (h + 1) * td, :]
        key = k_ref[b, a, h * td : (h + 1) * td, :]
        scores = jnp.where(causal, dot(key, query), 0.0).astype(BF16)
        right[u] = jnp.concatenate([scores, query], axis=0)

    def gather(u):
        a, b, h = units[u]
        s = b * memories + i * part + a
        for m in range(memories):
            j = 2 * ROWS + h * memories + m
            rows = slice(m * hd, (m + 1) * hd)
            state = lhs_ref[b, a, h, rows, td:].astype(F32) + st_scr[h, rows, :] * fac_ref[s, j : j + 1, :]
            left = jnp.concatenate([lhs_ref[b, a, h, rows, :td], state.astype(BF16)], axis=1)
            acc_scr[u, rows, :] = dot(left, right[u])

    def finish(u):
        a, b, h = units[u]
        s = b * memories + i * part + a
        mixed = None
        for m in range(memories):
            j = h * memories + m
            read = acc_scr[u, m * hd : (m + 1) * hd, :] * fac_ref[s, j : j + 1, :]
            mean = jnp.sum(read * read, axis=0, keepdims=True) * (1.0 / hd)
            term = read * (lax.rsqrt(mean + 1e-06) * fac_ref[s, ROWS + j : ROWS + j + 1, :])
            mixed = term if mixed is None else mixed + term
        out_ref[a, b, h * td : (h + 1) * td, :] = (mixed * gain_scr[h]).astype(BF16).T

    count = len(units)
    for u in range(count + 8):
        if u < count:
            score(u)
        if 0 <= u - 4 < count:
            gather(u - 4)
        if 0 <= u - 8 < count:
            finish(u - 8)


def readout(q, kv, lhs, factors, state, gain, lo, hl, memories, td):
    g, _, hd = q.shape
    part = max(1, math.gcd(memories, 8 // math.gcd(lo, 8)))
    q = q.reshape(memories, lo, hl * td, hd)
    tokens = pl.BlockSpec((part, lo, hl * td, hd), lambda i: (i, 0, 0, 0))
    out = pl.pallas_call(
        functools.partial(readout_kernel, hl, memories, lo, td),
        grid=(memories // part,),
        in_specs=[
            tokens,
            pl.BlockSpec((lo, part, hl * td, hd), lambda i: (0, i, 0, 0)),
            pl.BlockSpec((lo, part) + lhs.shape[1:], lambda i: (0, i, 0, 0, 0)),
            pl.BlockSpec(factors.shape, lambda i: (0, 0, 0)),
            pl.BlockSpec(state.shape, lambda i: (0, 0, 0)),
            pl.BlockSpec(gain.shape, lambda i: (0, 0)),
        ],
        out_specs=tokens,
        out_shape=jax.ShapeDtypeStruct(q.shape, BF16),
        scratch_shapes=[
            pltpu.VMEM(state.shape, F32),
            pltpu.VMEM((hl, hd, td), F32),
            pltpu.VMEM((part * lo * hl, memories * hd, td), F32),
        ],
        compiler_params=PARAMS,
        cost_estimate=pl.CostEstimate(
            flops=8 * g * td * hl * memories * hd * hd, bytes_accessed=kv.size * 10, transcendentals=0
        ),
        name="readout",
    )(
        q,
        kv.reshape((lo, memories) + kv.shape[1:]),
        lhs.reshape((lo, memories) + lhs.shape[1:]),
        factors,
        state,
        gain,
    )
    return out.reshape(g, hl * td, hd)


def entering_state(state, total, groups, hl, memories):
    if groups == 1:
        return jnp.zeros_like(state)
    state = lax.ppermute(state, "hi", [(i, i + 1) for i in range(groups - 1)])
    if groups == 2:
        return state
    factor = lax.ppermute(total[:, :1], "hi", [(i, i + 1) for i in range(groups - 1)])

    def spread(f):
        wide = jnp.broadcast_to(f.reshape(hl, memories, 1), (hl, memories, state.shape[2]))
        return wide.reshape(hl, state.shape[1], 1)

    held = state.astype(F32)
    step = 1
    while step < groups - 1:
        pairs = [(i, i + step) for i in range(groups - step)]
        earlier = lax.ppermute(held.astype(BF16), "hi", pairs).astype(F32)
        earlier_factor = lax.ppermute(factor, "hi", pairs)
        held = held + spread(factor) * earlier
        factor = factor * earlier_factor
        step *= 2
    return held.astype(BF16)


def shards(queries, keys, values, log_decay, routes, route_weight, gain):
    td, heads, hd = queries.shape[1:]
    memories = lax.axis_size("mem")
    lo = lax.axis_size("lo")
    groups = lax.axis_size("hi")
    g = memories * lo
    hl = heads // g
    assert hl <= META - RATES and hl * memories == ROWS
    kv_send, q_send = pack(
        keys[0],
        values[0],
        queries[0],
        log_decay[0].T,
        routes[0].T,
        route_weight[0].T,
        lo,
        memories,
        hl,
    )
    kv_send = kv_send.reshape(g, 2 * hl * td + META, hd)
    kv = lax.all_to_all(kv_send, ("lo", "mem"), split_axis=0, concat_axis=0, tiled=True)
    q = lax.all_to_all(q_send, ("mem", "lo"), split_axis=0, concat_axis=0, tiled=True)
    state, total = local_state(kv, hl, memories, td)
    entering = entering_state(state, total, groups, hl, memories)
    factors = chunk_factors(kv, hl, memories, td)
    lhs = chunk_states(kv, factors, hl, memories, td)
    out = readout(q, kv, lhs, factors, entering, gain.reshape(heads, hd), lo, hl, memories, td)
    back = lax.all_to_all(out, ("mem", "lo"), split_axis=0, concat_axis=0, tiled=True)
    return back.reshape(heads, td, hd).transpose(1, 0, 2)[None]


def solution(mesh):
    memories, blocks = mesh.shape["mem"], mesh.shape["ctx"]
    def call(queries, keys, values, log_decay, routes, route_weight, gain):
        heads = queries.shape[2]
        lo = max(
            s
            for s in range(1, max(1, blocks // 2) + 1)
            if blocks % s == 0 and heads % (memories * s) == 0
        )
        split = Mesh(mesh.devices.reshape(memories, blocks // lo, lo), ("mem", "hi", "lo"))
        tokens = P(("hi", "lo"), "mem")
        return jax.shard_map(
            shards,
            mesh=split,
            in_specs=(tokens,) * 6 + (P(),),
            out_specs=tokens,
            check_vma=False,
        )(queries, keys, values, log_decay, routes, route_weight, gain)

    return call
```
